128 devices in a mesh: row: 8 (over z, core), col: 16 (over x, y).
Axes of the slice: x: 4, y: 4, z: 4, core: 2. Of those that a mesh axis runs over, the one named last changes fastest.
Arguments:
- spectra: bfloat16 [24576, 144, 128], P(('row', 'col')), may hold values from -30 to 30
- station_ids: int32 [24576], P(('row', 'col')), may hold values from 0 to 12287, as said below
- counts: int32 [128], P(('row', 'col')), may hold values from 0 to 192, as said below
Outputs:
- cross_spectra: bfloat16 [3, 2, 12288, 12288], P(None, None, 'row', 'col')
The draws below stay inside these ranges and needn't reach their ends.
Inputs may be any that keep to these rules, and one draw needn't show every extreme that they name: `station_ids`: the live slots of all readers name every station exactly once; slots at or past a reader's count hold arbitrary station numbers and carry no data. The counts sum to 12288. Among the live slots of one reader, at most 2 name stations of one block h * 96 to h * 96 + 95, and that number is reached in every draw.
All inputs are finite; a program needn't handle non-finite values.
Results may differ from the reference program's by a relative error of at most 0.001.
Values may be sent and summed in bfloat16 or wider, within the bound.
A program may use at most 128 MiB of HBM per device.

```python
import math
import jax
import jax.numpy as jnp
from jax import lax

SD = 96
SEG = 144
NB = 64
READERS = 128
CAP = 192
STATIONS = 12288
N_ROW = 8
N_COL = 16


def layout_plan(key):
    base_key = jax.random.fold_in(key, 17)
    subkeys = jax.random.split(base_key, 5)
    pair_count = READERS // 2
    merged = jax.random.randint(subkeys[0], (pair_count,), 0, 2)
    forced = jax.random.randint(subkeys[1], (), 0, pair_count)
    merged = jnp.where(jnp.arange(pair_count) == forced, 1, merged)
    receiver_side = jax.random.randint(subkeys[2], (pair_count,), 0, 2)
    station = jnp.arange(STATIONS, dtype=jnp.int32)
    within_block = station % SD
    reader_of = (station // SD + within_block // 2 + within_block % 2 * (READERS // 2)) % READERS
    pair_index = reader_of // 2
    reader_of = jnp.where(merged[pair_index] == 1, 2 * pair_index + receiver_side[pair_index], reader_of)
    counts = jax.ops.segment_sum(jnp.ones_like(station), reader_of, num_segments=READERS)
    shuffle = jax.random.permutation(subkeys[3], STATIONS).astype(jnp.int32)
    ordered = jnp.argsort(reader_of * STATIONS + shuffle, stable=True).astype(jnp.int32)
    offsets = jnp.cumsum(counts) - counts
    slot_index = jnp.arange(CAP, dtype=jnp.int32)
    position = offsets[:, None] + slot_index[None, :]
    is_live = slot_index[None, :] < counts[:, None]
    filler = jax.random.randint(subkeys[4], (READERS, CAP), 0, STATIONS)
    station_list = jnp.where(is_live, ordered[jnp.clip(position, 0, STATIONS - 1)], filler)
    return (station_list.reshape(-1).astype(jnp.int32), counts.astype(jnp.int32))


def draw_station_ids(key, part):
    return layout_plan(key)[0]


def draw_counts(key, part):
    return layout_plan(key)[1]


def draw_spectra(key, part):
    subkeys = jax.random.split(jax.random.fold_in(key, 29), 3)
    full_shape = (READERS * CAP, SEG, 2 * NB)
    row_scale = jnp.exp(jax.random.uniform(subkeys[0], (READERS * CAP, SEG, 1), jnp.float32, math.log(0.3), math.log(3.0)))
    bin_scale = jnp.exp(jax.random.uniform(subkeys[1], (READERS * CAP, SEG, NB), jnp.float32, math.log(0.5), math.log(2.0)))
    bin_scale = jnp.concatenate([bin_scale, bin_scale], axis=2)
    noise = jnp.clip(jax.random.normal(subkeys[2], full_shape, jnp.float32), -4.0, 4.0)
    return (noise * row_scale * bin_scale).astype(jnp.bfloat16)


def setup_inputs(seed: int = 0) -> dict:
    arg_keys = jax.random.split(jax.random.key(seed), 4)
    spectra = draw_spectra(jax.random.fold_in(arg_keys[3], 71), 0)
    station_ids = draw_station_ids(jax.random.fold_in(arg_keys[3], 71), 0)
    counts = draw_counts(jax.random.fold_in(arg_keys[3], 71), 0)
    return dict(spectra=spectra, station_ids=station_ids, counts=counts)


power_floor = 0.25

def whiten(raw):
    values = raw.astype(jnp.float32)
    band = values.shape[2] // 2
    real_part = values[:, :, :band]
    imag_part = values[:, :, band:]
    energy = real_part * real_part + imag_part * imag_part
    pieces = []
    for bin_index in range(3):
        lower = bin_index * band // 4
        averaged = lax.optimization_barrier(jnp.mean(energy[:, :, lower:lower + band // 2], axis=2))
        amplitude = jnp.sqrt(jnp.maximum(averaged, power_floor))
        center = lower + band // 4
        pieces.append(real_part[:, :, center] / amplitude)
        pieces.append(imag_part[:, :, center] / amplitude)
    return jnp.concatenate(pieces, axis=1)

def reference(spectra, station_ids, counts):
    blocks = spectra.reshape(READERS, CAP, SEG, 2 * NB)
    id_blocks = station_ids.reshape(READERS, CAP)
    slot_index = jnp.arange(CAP, dtype=jnp.int32)

    def absorb(white, inputs):
        raw, station_list, live_count = inputs
        whitened = whiten(raw)
        target = jnp.where(slot_index < live_count, station_list, STATIONS).astype(jnp.int32)
        return (white.at[target].set(whitened, mode='drop'), None)
    start = jnp.zeros((STATIONS, 6 * SEG), jnp.float32)
    white, unused = lax.scan(absorb, start, (blocks, id_blocks, counts))
    column = jnp.arange(STATIONS, dtype=jnp.int32)
    sigma = (column // SD % N_ROW * N_COL + column // (SD * N_ROW)) * SD + column % SD
    column_white = white[sigma]
    norm_factor = 1.0 / math.sqrt(SEG)
    row_block = STATIONS // N_ROW
    outputs = []
    for bin_index in range(3):
        real_imag = white[:, bin_index * 2 * SEG:(bin_index + 1) * 2 * SEG]
        rotated = jnp.concatenate([real_imag[:, SEG:], -real_imag[:, :SEG]], axis=1)
        other = column_white[:, bin_index * 2 * SEG:(bin_index + 1) * 2 * SEG]

        def tile_rows(pair):
            stacked = jnp.concatenate([pair[0], pair[1]], axis=0)
            product = lax.dot_general(stacked, other, (((1,), (1,)), ((), ())), precision=lax.Precision.HIGHEST, preferred_element_type=jnp.float32)
            return (product * norm_factor).astype(jnp.bfloat16).reshape(2, row_block, STATIONS)
        tiles = lax.map(tile_rows, (real_imag.reshape(N_ROW, row_block, 2 * SEG), rotated.reshape(N_ROW, row_block, 2 * SEG)))
        outputs.append(jnp.transpose(tiles, (1, 0, 2, 3)).reshape(2, STATIONS, STATIONS))
    return jnp.stack(outputs, axis=0)
```

```python
import functools
import math

import jax
import jax.numpy as jnp
from jax import lax
from jax.experimental import pallas as pl
from jax.experimental.pallas import tpu as pltpu
from jax.sharding import PartitionSpec as P

def whiten_kernel(ids_ref, counts_ref, x_ref, out_ref, used_ref):
    step = pl.program_id(0)
    group = x_ref.shape[0]
    homes = used_ref.shape[0]
    dummy = 2 * homes

    @pl.when(step == 0)
    def _():
        out_ref[...] = jnp.zeros_like(out_ref)
        def clear(i, c):
            used_ref[i] = 0
            return c
        lax.fori_loop(0, homes, clear, 0)

    x = x_ref[...]
    x = jnp.concatenate([x[:, :128].reshape(group * 128, 128), x[:, 128:].reshape(group * 16, 128)], axis=0)
    xf = x.astype(jnp.float32)
    energy = xf * xf
    high = energy.astype(jnp.bfloat16)
    low = (energy - high.astype(jnp.float32)).astype(jnp.bfloat16)
    q = lax.broadcasted_iota(jnp.int32, (8, 128), 0)
    lane = lax.broadcasted_iota(jnp.int32, (8, 128), 1)
    start = (q // 2) * 16
    inside = (q < 6) & ((lane & 63) >= start) & ((lane & 63) < start + 32)
    window = jnp.where(inside, 1.0, 0.0).astype(jnp.bfloat16)
    center = jnp.where((q < 6) & (lane == start + 16 + (q & 1) * 64), 1.0, 0.0).astype(jnp.bfloat16)
    contract = (((1,), (1,)), ((), ()))
    total = lax.dot_general(jnp.concatenate([window, window], axis=1), jnp.concatenate([high, low], axis=1),
                            contract, preferred_element_type=jnp.float32)
    values = lax.dot_general(center, x, contract, preferred_element_type=jnp.float32)
    white = values * lax.rsqrt(jnp.maximum(total * (1.0 / 32), 0.25))

    sub = lax.broadcasted_iota(jnp.int32, (8, 128), 0)
    chunk = lax.broadcasted_iota(jnp.int32, (8, 128), 1) // 16
    for part in range(group // 8):
        base = group * 128 + part * 128
        tail = white[:, base:base + 128]
        turned = jnp.zeros_like(tail)
        for d in range(8):
            piece = jnp.where(((chunk - sub) & 7) == d, tail, 0.0)
            if d:
                piece = pltpu.roll(pltpu.roll(piece, 128 - 16 * d, 1), d, 0)
            turned = turned + piece
        for k in range(8):
            j = part * 8 + k
            slot = step * group + j
            station = ids_ref[slot]
            home = (station * 43691) >> 22
            live = slot < counts_ref[0]
            seen = used_ref[home]
            used_ref[home] = jnp.where(live, seen + 1, seen)
            place = jnp.where(live, home * 2 + seen, dummy)
            mark = (station - home * 96 + 1).astype(jnp.float32)
            tile = jnp.where(sub < 6, white[:, j * 128:(j + 1) * 128],
                             jnp.where(sub == 6, jnp.broadcast_to(turned[k:k + 1], (8, 128)), mark))
            out_ref[place] = tile

def whiten_pack(spectra, ids, counts, homes, group=8):
    slots, segs, width = spectra.shape
    return pl.pallas_call(
        whiten_kernel,
        out_shape=jax.ShapeDtypeStruct((2 * homes + 8, 8, 128), jnp.float32),
        grid=(slots // group,),
        in_specs=[pl.BlockSpec(memory_space=pltpu.SMEM), pl.BlockSpec(memory_space=pltpu.SMEM),
                  pl.BlockSpec((group, segs, width), lambda i: (i, 0, 0))],
        out_specs=pl.BlockSpec((2 * homes + 8, 8, 128), lambda i: (0, 0, 0)),
        scratch_shapes=[pltpu.SMEM((homes,), jnp.int32)],
        name="whiten_pack",
    )(ids, counts, spectra)


MESH = pl.DeviceIdType.MESH
RING = 4
X, Y = 0, 1


def arrival(half, ox, oy, q):
    axes = (X, Y) if half == 0 else (Y, X)
    off = {X: ox, Y: oy}
    for axis in (axes[1], axes[0]):
        o = off[axis]
        if o:
            return (axis, 1) if o == 3 or (o == 2 and q == 0) else (axis, -1)
    return None


def row_plan():
    items = []
    for half in (0, 1):
        axes = (X, Y) if half == 0 else (Y, X)
        for ox in range(RING):
            for oy in range(RING):
                off = {X: ox, Y: oy}
                for q in (0, 1):
                    for level, axis in enumerate(axes):
                        if level == 0 and off[axes[1]]:
                            continue
                        o = off[axis]
                        for direction in (1, -1):
                            first = o == 0
                            onward = (o == 3 and direction == 1 and q == 0) or (o == 1 and direction == -1 and q == 1)
                            if first or onward:
                                depth = (2 if level == 0 else 0) + (1 if first else 0)
                                items.append(((half, ox, oy, q, axis, direction), depth))
    ready = {(half, 0, 0, q): 0 for half in (0, 1) for q in (0, 1)}
    busy = {}
    order = []
    left = list(items)
    time = 0
    while left:
        for link in ((X, 1), (X, -1), (Y, 1), (Y, -1)):
            best = None
            for entry in left:
                item, depth = entry
                if item[4:] == link and ready.get(item[:4], 99999) <= time:
                    key = (-depth, ready[item[:4]])
                    if best is None or key < best[0]:
                        best = (key, entry)
            if best is not None:
                entry = best[1]
                left.remove(entry)
                half, ox, oy, q, axis, direction = entry[0]
                order.append(entry[0])
                there = (half, (ox - direction) % RING if axis == X else ox,
                         (oy - direction) % RING if axis == Y else oy, q)
                assert arrival(*there) == (axis, direction) and there not in ready
                ready[there] = time + 2
        time += 1
    return order


def exchange_kernel(packed_ref, rows_ref, cols_ref, recv_ref, a2a_send, a2a_recv, own_sem,
                    row_send, row_recv, col_send, col_recv):
    r = lax.axis_index("row")
    c = lax.axis_index("col")
    nr, nc = lax.axis_size("row"), lax.axis_size("col")
    x, y = c // RING, c % RING
    n = nr * nc
    me = r * nc + c

    barrier = pltpu.get_barrier_semaphore()

    def peer(d):
        p = (me + d) % n
        return p, (p // nc, p % nc)

    def greet(d, carry):
        pl.semaphore_signal(barrier, inc=1, device_id=peer(d)[1], device_id_type=MESH)
        return carry
    lax.fori_loop(1, n, greet, 0)
    pl.semaphore_wait(barrier, n - 1)

    def slots(p):
        return pl.ds(pl.multiple_of(p * 16, 16), 16)

    def post(d, carry):
        p, where = peer(d)
        pltpu.make_async_remote_copy(packed_ref.at[slots(p)], recv_ref.at[slots(me)], a2a_send, a2a_recv,
                                     device_id=where, device_id_type=MESH).start()
        return carry
    lax.fori_loop(1, n, post, 0)
    mine = pltpu.make_async_copy(packed_ref.at[slots(me)], recv_ref.at[slots(me)], own_sem)
    mine.start()
    mine.wait()
    others = pl.ds(0, 16 * (n - 1))
    pltpu.make_async_copy(recv_ref.at[others], recv_ref.at[others], a2a_recv).wait()

    total = 2 * n
    sd = rows_ref.shape[2]
    mark = recv_ref[pl.ds(7, total, stride=8), :]
    lane = lax.broadcasted_iota(jnp.int32, mark.shape, 1)
    hit = jnp.where(mark == (lane + 1).astype(jnp.float32), 1.0, 0.0)
    pick = jnp.transpose(hit)[:sd].astype(jnp.bfloat16)
    for k in range(7):
        values = recv_ref[pl.ds(k, total, stride=8), :]
        high = values.astype(jnp.bfloat16)
        low = (values - high.astype(jnp.float32)).astype(jnp.bfloat16)
        placed = jnp.dot(pick, jnp.concatenate([high, low], axis=1),
                         preferred_element_type=jnp.float32).astype(jnp.bfloat16)
        for half in (0, 1):
            piece = placed[:, half * 128:(half + 1) * 128]
            rows_ref[half, c, :, k * 128:(k + 1) * 128] = piece
            cols_ref[half, r, :, k * 128:(k + 1) * 128] = piece

    part = sd // 2
    row_sem = {}

    def row_copy(item):
        half, ox, oy, q, axis, direction = item
        source = (x + ox) % RING * RING + (y + oy) % RING
        ref = rows_ref.at[half, source, pl.ds(q * part, part)]
        tx, ty = (x + direction) % RING, (y + direction) % RING
        target = (tx * RING + y) if axis == X else (x * RING + ty)
        there = (half, (ox - direction) % RING if axis == X else ox,
                 (oy - direction) % RING if axis == Y else oy, q)
        index = row_sem.setdefault(there, len(row_sem))
        return pltpu.make_async_remote_copy(ref, ref, row_send, row_recv.at[index],
                                            device_id=(r, target), device_id_type=MESH)

    def row_wait(half, ox, oy, q):
        source = (x + ox) % RING * RING + (y + oy) % RING
        ref = rows_ref.at[half, source, pl.ds(q * part, part)]
        pltpu.make_async_copy(ref, ref, row_recv.at[row_sem[(half, ox, oy, q)]]).wait()

    z, core = r // 2, r % 2
    col_sem = {}

    def col_copy(oz, q, link):
        source = (z + oz) % RING * 2 + core
        ref = cols_ref.at[:, source, pl.ds(q * part, part)]
        if link == 0:
            target = z * 2 + (1 - core)
            there = ("core", oz, q)
        else:
            target = (z + link) % RING * 2 + core
            there = ("z", (oz - link) % RING, q)
        index = col_sem.setdefault(there, len(col_sem))
        return pltpu.make_async_remote_copy(ref, ref, col_send, col_recv.at[index],
                                            device_id=(target, c), device_id_type=MESH)

    def col_wait(kind, oz, q):
        source = (z + oz) % RING * 2 + (core if kind == "z" else 1 - core)
        ref = cols_ref.at[:, source, pl.ds(q * part, part)]
        pltpu.make_async_copy(ref, ref, col_recv.at[col_sem[(kind, oz, q)]]).wait()

    plan = row_plan()
    first = [i for i in plan if i[1] == 0 and i[2] == 0]
    for item in plan:
        row_sem.setdefault((item[0], (item[1] - item[5]) % RING if item[4] == X else item[1],
                            (item[2] - item[5]) % RING if item[4] == Y else item[2], item[3]), len(row_sem))
    for q in (0, 1):
        col_copy(0, q, 1).start()
        col_copy(0, q, -1).start()
    for item in first:
        row_copy(item).start()
    for q in (0, 1):
        col_copy(0, q, 0).start()

    col_steps = [
        ("z", 3, 0, (1, 0)), ("z", 1, 1, (-1, 0)), ("z", 3, 1, (0,)), ("z", 1, 0, (0,)),
        ("z", 2, 0, (0,)), ("z", 2, 1, (0,)),
    ]
    waited = set()
    rest = [i for i in plan if i not in first]
    for number, item in enumerate(rest):
        if number % 4 == 3 and col_steps:
            kind, oz, q, links = col_steps.pop(0)
            col_wait(kind, oz, q)
            for link in links:
                col_copy(oz, q, link).start()
        chunk = item[:4]
        if chunk not in waited:
            row_wait(*chunk)
            waited.add(chunk)
        row_copy(item).start()
    for oz in range(RING):
        for q in (0, 1):
            col_wait("core", oz, q)
    for chunk in row_sem:
        if chunk not in waited:
            row_wait(*chunk)
    sent = packed_ref.at[others]
    pltpu.make_async_copy(sent, sent, a2a_send).wait()
    sent = rows_ref.at[:, pl.ds(0, nc - 1)]
    pltpu.make_async_copy(sent, sent, row_send).wait()
    sent = cols_ref.at[:, pl.ds(0, nr - 1)]
    pltpu.make_async_copy(sent, sent, col_send).wait()


def exchange(packed, nr, nc, sd):
    n = nr * nc
    dma = pltpu.SemaphoreType.DMA
    return pl.pallas_call(
        exchange_kernel,
        out_shape=(jax.ShapeDtypeStruct((2, nc, sd, 896), jnp.bfloat16),
                   jax.ShapeDtypeStruct((2, nr, sd, 896), jnp.bfloat16)),
        in_specs=[pl.BlockSpec(memory_space=pltpu.VMEM)],
        out_specs=(pl.BlockSpec(memory_space=pltpu.VMEM), pl.BlockSpec(memory_space=pltpu.VMEM)),
        scratch_shapes=[pltpu.VMEM((16 * n, 128), jnp.float32), dma, dma, dma,
                        dma, dma((60,)), dma, dma((14,))],
        compiler_params=pltpu.CompilerParams(collective_id=0, has_side_effects=True),
        name="exchange",
    )(packed)


def spread_tail(first, second, third, shift):
    lane = lax.broadcasted_iota(jnp.int32, first.shape, 1)
    out = jnp.where(lane < 32, pltpu.roll(first, (128 - shift) % 128, 1), 0.0)
    out = jnp.where((lane >= 32) & (lane < 64), pltpu.roll(second, (160 - shift) % 128, 1), out)
    return jnp.where((lane >= 64) & (lane < 96), pltpu.roll(third, (192 - shift) % 128, 1), out)

def prepare(cols_ref, rhs_ref):
    blocks, sd = cols_ref.shape[1], cols_ref.shape[2]
    n = blocks * sd
    lane = lax.broadcasted_iota(jnp.int32, (sd, 128), 1)
    for b in range(blocks):
        h = cols_ref[0, b]
        l = cols_ref[1, b]
        ht = h[:, 768:].astype(jnp.float32)
        lt = l[:, 768:].astype(jnp.float32)
        for f in range(3):
            hr, hi = h[:, 256 * f:256 * f + 128], h[:, 256 * f + 128:256 * f + 256]
            lr, li = l[:, 256 * f:256 * f + 128], l[:, 256 * f + 128:256 * f + 256]
            t = spread_tail(ht, lt, ht, 32 * f)
            u = jnp.where((lane & 16) == 0, -pltpu.roll(t, 112, 1), pltpu.roll(t, 16, 1))
            rhs_ref[f, b * sd:(b + 1) * sd] = jnp.concatenate([hr, hi, lr, li, hr, hi, t.astype(jnp.bfloat16)], axis=1)
            rhs_ref[f, n + b * sd:n + (b + 1) * sd] = jnp.concatenate([-hi, hr, -li, lr, -hi, hr, u.astype(jnp.bfloat16)], axis=1)

def pair_kernel(norm, cols_ref, rows_ref, out_ref, rhs_ref):
    @pl.when((pl.program_id(0) == 0))
    def _():
        prepare(cols_ref, rhs_ref)
    gb, sd = rows_ref.shape[1], rows_ref.shape[2]
    n = rhs_ref.shape[1] // 2
    h = rows_ref[0].reshape(gb * sd, -1)
    l = rows_ref[1].reshape(gb * sd, -1)
    ht = h[:, 768:].astype(jnp.float32)
    lt = l[:, 768:].astype(jnp.float32)
    for f in range(3):
        t = spread_tail(ht, ht, lt, 32 * f).astype(jnp.bfloat16)
        hm = h[:, 256 * f:256 * f + 256]
        lhs = jnp.concatenate([hm, hm, l[:, 256 * f:256 * f + 256], t], axis=1)
        p = lax.dot_general(lhs, rhs_ref[f], (((1,), (1,)), ((), ())), preferred_element_type=jnp.float32)
        p = (p * norm).astype(jnp.bfloat16)
        out_ref[f, 0] = p[:, :n]
        out_ref[f, 1] = p[:, n:]

def pair_products(rows, cols, norm, gb):
    _, nb, sd, width = rows.shape
    cb = cols.shape[1]
    n = cb * sd
    return pl.pallas_call(
        functools.partial(pair_kernel, norm),
        out_shape=jax.ShapeDtypeStruct((3, 2, nb * sd, n), jnp.bfloat16),
        grid=(nb // gb,),
        in_specs=[pl.BlockSpec((2, cb, sd, width), lambda i: (0, 0, 0, 0), pipeline_mode=pl.Buffered(1)),
                  pl.BlockSpec((2, gb, sd, width), lambda i: (0, i, 0, 0))],
        out_specs=pl.BlockSpec((3, 2, gb * sd, n), lambda i: (0, 0, i, 0)),
        scratch_shapes=[pltpu.VMEM((3, 2 * n, width), jnp.bfloat16)],
        name="pair_products",
    )(cols, rows)


def shards(spectra, station_ids, counts):
    row_count = lax.axis_size("row")
    column_count = lax.axis_size("col")
    readers = row_count * column_count
    slots, segments, _ = spectra.shape
    home_rows = slots // 2
    packed = whiten_pack(spectra, station_ids, counts, readers, group=48)
    packed = packed.reshape(-1, 128)
    rows, cols = exchange(packed, row_count, column_count, home_rows)
    return pair_products(rows, cols, 1.0 / math.sqrt(segments), 4)


def solution(mesh):
    in_specs = (P(("row", "col"), None, None), P(("row", "col")), P(("row", "col")))
    out_specs = P(None, None, "row", "col")
    return jax.shard_map(shards, mesh=mesh, in_specs=in_specs, out_specs=out_specs, check_vma=False)
```

```python
import functools
import math

import jax
import jax.numpy as jnp
from jax import lax
from jax.experimental import pallas as pl
from jax.experimental.pallas import tpu as pltpu
from jax.sharding import PartitionSpec as P

def whiten_kernel(ids_ref, counts_ref, x_ref, out_ref, used_ref):
    first = pl.program_id(0) == 0
    step = pl.num_programs(0) - 1 - pl.program_id(0)
    group = x_ref.shape[0]
    homes = used_ref.shape[0]

    @pl.when(first)
    def _():
        out_ref[...] = jnp.zeros_like(out_ref)
        def clear(i, c):
            used_ref[i] = 0
            return c
        lax.fori_loop(0, homes, clear, 0)

    x = x_ref[...]
    x = jnp.concatenate([x[:, :128].reshape(group * 128, 128), x[:, 128:].reshape(group * 16, 128)], axis=0)
    xf = x.astype(jnp.float32)
    energy = xf * xf
    high = energy.astype(jnp.bfloat16)
    low = (energy - high.astype(jnp.float32)).astype(jnp.bfloat16)
    q = lax.broadcasted_iota(jnp.int32, (8, 128), 0)
    lane = lax.broadcasted_iota(jnp.int32, (8, 128), 1)
    start = (q // 2) * 16
    inside = (q < 6) & ((lane & 63) >= start) & ((lane & 63) < start + 32)
    window = jnp.where(inside, 1.0, 0.0).astype(jnp.bfloat16)
    center = jnp.where((q < 6) & (lane == start + 16 + (q & 1) * 64), 1.0, 0.0).astype(jnp.bfloat16)
    contract = (((1,), (1,)), ((), ()))
    total = lax.dot_general(jnp.concatenate([window, window], axis=1), jnp.concatenate([high, low], axis=1),
                            contract, preferred_element_type=jnp.float32)
    values = lax.dot_general(center, x, contract, preferred_element_type=jnp.float32)
    white = values * lax.rsqrt(jnp.maximum(total * (1.0 / 32), 0.25))

    sub = lax.broadcasted_iota(jnp.int32, (8, 128), 0)
    chunk = lax.broadcasted_iota(jnp.int32, (8, 128), 1) // 16
    for part in reversed(range(group // 8)):
        base = group * 128 + part * 128
        tail = white[:, base:base + 128]
        turned = jnp.zeros_like(tail)
        for d in range(8):
            piece = jnp.where(((chunk - sub) & 7) == d, tail, 0.0)
            if d:
                piece = pltpu.roll(pltpu.roll(piece, 128 - 16 * d, 1), d, 0)
            turned = turned + piece
        for k in reversed(range(8)):
            j = part * 8 + k
            slot = step * group + j
            station = ids_ref[slot]
            home = (station * 43691) >> 22
            live = slot < counts_ref[0]
            seen = used_ref[home]
            used_ref[home] = jnp.where(live, seen + 1, seen)
            place = jnp.where(live, seen * homes + home, 0)
            mark = (station - home * 96 + 1).astype(jnp.float32)
            tile = jnp.where(sub < 6, white[:, j * 128:(j + 1) * 128],
                             jnp.where(sub == 6, jnp.broadcast_to(turned[k:k + 1], (8, 128)), mark))
            out_ref[place] = jnp.where(live, tile, 0.0)

def whiten_pack(spectra, ids, counts, homes, group=8):
    slots, segs, width = spectra.shape
    return pl.pallas_call(
        whiten_kernel,
        out_shape=jax.ShapeDtypeStruct((2 * homes, 8, 128), jnp.float32),
        grid=(slots // group,),
        in_specs=[pl.BlockSpec(memory_space=pltpu.SMEM), pl.BlockSpec(memory_space=pltpu.SMEM),
                  pl.BlockSpec((group, segs, width), lambda i: (slots // group - 1 - i, 0, 0))],
        out_specs=pl.BlockSpec((2 * homes, 8, 128), lambda i: (0, 0, 0)),
        scratch_shapes=[pltpu.SMEM((homes,), jnp.int32)],
        compiler_params=pltpu.CompilerParams(vmem_limit_bytes=60 * 2**20),
        name="whiten_pack",
    )(ids, counts, spectra)


MESH = pl.DeviceIdType.MESH
RING = 4
X, Y = 0, 1


def arrival(half, ox, oy, q):
    axes = (X, Y) if half == 0 else (Y, X)
    off = {X: ox, Y: oy}
    for axis in (axes[1], axes[0]):
        o = off[axis]
        if o:
            return (axis, 1) if o == 3 or (o == 2 and q == 0) else (axis, -1)
    return None


def row_plan():
    items = []
    for half in (0, 1):
        axes = (X, Y) if half == 0 else (Y, X)
        for ox in range(RING):
            for oy in range(RING):
                off = {X: ox, Y: oy}
                for q in (0, 1):
                    for level, axis in enumerate(axes):
                        if level == 0 and off[axes[1]]:
                            continue
                        o = off[axis]
                        for direction in (1, -1):
                            first = o == 0
                            onward = (o == 3 and direction == 1 and q == 0) or (o == 1 and direction == -1 and q == 1)
                            if first or onward:
                                depth = (2 if level == 0 else 0) + (1 if first else 0)
                                items.append(((half, ox, oy, q, axis, direction), depth))
    ready = {(half, 0, 0, q): 0 for half in (0, 1) for q in (0, 1)}
    busy = {}
    order = []
    left = list(items)
    time = 0
    while left:
        for link in ((X, 1), (X, -1), (Y, 1), (Y, -1)):
            best = None
            for entry in left:
                item, depth = entry
                if item[4:] == link and ready.get(item[:4], 99999) <= time:
                    key = (-depth, ready[item[:4]])
                    if best is None or key < best[0]:
                        best = (key, entry)
            if best is not None:
                entry = best[1]
                left.remove(entry)
                half, ox, oy, q, axis, direction = entry[0]
                order.append(entry[0])
                there = (half, (ox - direction) % RING if axis == X else ox,
                         (oy - direction) % RING if axis == Y else oy, q)
                assert arrival(*there) == (axis, direction) and there not in ready
                ready[there] = time + 2
        time += 1
    return order


def exchange_kernel(packed_ref, rows_ref, cols_ref, mid0_ref, mid1_ref, recv0_ref, recv1_ref, own_sem, hop_send, hop_recv,
                    row_send, row_recv, col_send, col_recv):
    r = lax.axis_index("row")
    c = lax.axis_index("col")
    nr, nc = lax.axis_size("row"), lax.axis_size("col")
    x, y = c // RING, c % RING

    barrier = pltpu.get_barrier_semaphore()
    row_peers = [(r + d) % nr for d in range(1, nr)]
    col_peers = [(c + d) % nc for d in range(1, nc)]
    for p in row_peers:
        pl.semaphore_signal(barrier, inc=1, device_id=(p, c), device_id_type=MESH)
    for p in col_peers:
        pl.semaphore_signal(barrier, inc=1, device_id=(r, p), device_id_type=MESH)
    pl.semaphore_wait(barrier, nr + nc - 2)

    def send(source, target, where, k):
        pltpu.make_async_remote_copy(source, target, hop_send.at[k], hop_recv.at[k],
                                     device_id=where, device_id_type=MESH).start()

    def keep(source, target, k):
        pltpu.make_async_copy(source, target, own_sem.at[k]).start()

    def arrive(ref, count, local, k):
        others = ref.at[pl.ds(0, count)]
        pltpu.make_async_copy(others, others, hop_recv.at[k]).wait()
        pltpu.make_async_copy(local, local, own_sem.at[k]).wait()

    for p in col_peers:
        send(packed_ref.at[1, :, p], mid1_ref.at[c], (r, p), 1)
    for p in row_peers:
        send(packed_ref.at[0, p], mid0_ref.at[r], (p, c), 0)
    keep(packed_ref.at[0, r], mid0_ref.at[r], 0)
    keep(packed_ref.at[1, :, c], mid1_ref.at[c], 1)
    arrive(mid0_ref, nr - 1, mid0_ref.at[r], 0)
    for p in col_peers:
        send(mid0_ref.at[:, p], recv0_ref.at[c], (r, p), 2)
    keep(mid0_ref.at[:, c], recv0_ref.at[c], 2)
    arrive(mid1_ref, nc - 1, mid1_ref.at[c], 1)
    for p in row_peers:
        send(mid1_ref.at[:, p], recv1_ref.at[r], (p, c), 3)
    keep(mid1_ref.at[:, r], recv1_ref.at[r], 3)
    arrive(recv0_ref, nc - 1, recv0_ref.at[c], 2)
    arrive(recv1_ref, nr - 1, recv1_ref.at[r], 3)

    half_slots = nr * nc
    sd = rows_ref.shape[2]
    flat = [ref.reshape(half_slots * 8, 128) for ref in (recv0_ref, recv1_ref)]

    def plane(k):
        return jnp.concatenate([ref[pl.ds(k, half_slots, stride=8), :] for ref in flat], axis=0)

    mark = plane(7)
    lane = lax.broadcasted_iota(jnp.int32, mark.shape, 1)
    hit = jnp.where(mark == (lane + 1).astype(jnp.float32), 1.0, 0.0)
    pick = jnp.transpose(hit)[:sd].astype(jnp.bfloat16)
    for k in range(7):
        values = plane(k)
        high = values.astype(jnp.bfloat16)
        low = (values - high.astype(jnp.float32)).astype(jnp.bfloat16)
        placed = jnp.dot(pick, jnp.concatenate([high, low], axis=1),
                         preferred_element_type=jnp.float32).astype(jnp.bfloat16)
        for half in (0, 1):
            piece = placed[:, half * 128:(half + 1) * 128]
            rows_ref[half, c, :, k * 128:(k + 1) * 128] = piece
            cols_ref[half, r, :, k * 128:(k + 1) * 128] = piece

    part = sd // 2
    row_sem = {}

    def row_copy(item):
        half, ox, oy, q, axis, direction = item
        source = (x + ox) % RING * RING + (y + oy) % RING
        ref = rows_ref.at[half, source, pl.ds(q * part, part)]
        tx, ty = (x + direction) % RING, (y + direction) % RING
        target = (tx * RING + y) if axis == X else (x * RING + ty)
        there = (half, (ox - direction) % RING if axis == X else ox,
                 (oy - direction) % RING if axis == Y else oy, q)
        index = row_sem.setdefault(there, len(row_sem))
        return pltpu.make_async_remote_copy(ref, ref, row_send, row_recv.at[index],
                                            device_id=(r, target), device_id_type=MESH)

    def row_wait(half, ox, oy, q):
        source = (x + ox) % RING * RING + (y + oy) % RING
        ref = rows_ref.at[half, source, pl.ds(q * part, part)]
        pltpu.make_async_copy(ref, ref, row_recv.at[row_sem[(half, ox, oy, q)]]).wait()

    z, core = r // 2, r % 2
    col_sem = {}

    def col_copy(oz, q, link):
        source = (z + oz) % RING * 2 + core
        ref = cols_ref.at[:, source, pl.ds(q * part, part)]
        if link == 0:
            target = z * 2 + (1 - core)
            there = ("core", oz, q)
        else:
            target = (z + link) % RING * 2 + core
            there = ("z", (oz - link) % RING, q)
        index = col_sem.setdefault(there, len(col_sem))
        return pltpu.make_async_remote_copy(ref, ref, col_send, col_recv.at[index],
                                            device_id=(target, c), device_id_type=MESH)

    def col_wait(kind, oz, q):
        source = (z + oz) % RING * 2 + (core if kind == "z" else 1 - core)
        ref = cols_ref.at[:, source, pl.ds(q * part, part)]
        pltpu.make_async_copy(ref, ref, col_recv.at[col_sem[(kind, oz, q)]]).wait()

    plan = row_plan()
    first = [i for i in plan if i[1] == 0 and i[2] == 0]
    for item in plan:
        row_sem.setdefault((item[0], (item[1] - item[5]) % RING if item[4] == X else item[1],
                            (item[2] - item[5]) % RING if item[4] == Y else item[2], item[3]), len(row_sem))
    for q in (0, 1):
        col_copy(0, q, 1).start()
        col_copy(0, q, -1).start()
    for item in first:
        row_copy(item).start()
    for q in (0, 1):
        col_copy(0, q, 0).start()

    col_steps = [
        ("z", 3, 0, (1, 0)), ("z", 1, 1, (-1, 0)), ("z", 3, 1, (0,)), ("z", 1, 0, (0,)),
        ("z", 2, 0, (0,)), ("z", 2, 1, (0,)),
    ]
    waited = set()
    rest = [i for i in plan if i not in first]
    for number, item in enumerate(rest):
        if number % 4 == 3 and col_steps:
            kind, oz, q, links = col_steps.pop(0)
            col_wait(kind, oz, q)
            for link in links:
                col_copy(oz, q, link).start()
        chunk = item[:4]
        if chunk not in waited:
            row_wait(*chunk)
            waited.add(chunk)
        row_copy(item).start()
    for oz in range(RING):
        for q in (0, 1):
            col_wait("core", oz, q)
    for chunk in row_sem:
        if chunk not in waited:
            row_wait(*chunk)
    for k, (ref, count) in enumerate([(mid0_ref, nr), (mid1_ref, nc), (recv0_ref, nc), (recv1_ref, nr)]):
        sent = ref.at[pl.ds(0, count - 1)]
        pltpu.make_async_copy(sent, sent, hop_send.at[k]).wait()
    sent = rows_ref.at[:, pl.ds(0, nc - 1)]
    pltpu.make_async_copy(sent, sent, row_send).wait()
    sent = cols_ref.at[:, pl.ds(0, nr - 1)]
    pltpu.make_async_copy(sent, sent, col_send).wait()


def exchange(packed, nr, nc, sd):
    dma = pltpu.SemaphoreType.DMA
    return pl.pallas_call(
        exchange_kernel,
        out_shape=(jax.ShapeDtypeStruct((2, nc, sd, 896), jnp.bfloat16),
                   jax.ShapeDtypeStruct((2, nr, sd, 896), jnp.bfloat16)),
        in_specs=[pl.BlockSpec(memory_space=pltpu.VMEM)],
        out_specs=(pl.BlockSpec(memory_space=pltpu.VMEM), pl.BlockSpec(memory_space=pltpu.VMEM)),
        scratch_shapes=[pltpu.VMEM((nr, nc, 8, 128), jnp.float32), pltpu.VMEM((nc, nr, 8, 128), jnp.float32),
                        pltpu.VMEM((nc, nr, 8, 128), jnp.float32), pltpu.VMEM((nr, nc, 8, 128), jnp.float32),
                        dma((4,)), dma((4,)), dma((4,)), dma, dma((60,)), dma, dma((14,))],
        compiler_params=pltpu.CompilerParams(collective_id=0, has_side_effects=True, vmem_limit_bytes=16 * 2**20),
        name="exchange",
    )(packed)


def spread_tail(first, second, third, shift):
    lane = lax.broadcasted_iota(jnp.int32, first.shape, 1)
    out = jnp.where(lane < 32, pltpu.roll(first, (128 - shift) % 128, 1), 0.0)
    out = jnp.where((lane >= 32) & (lane < 64), pltpu.roll(second, (160 - shift) % 128, 1), out)
    return jnp.where((lane >= 64) & (lane < 96), pltpu.roll(third, (192 - shift) % 128, 1), out)

def prepare(cols_ref, rhs_ref):
    blocks, sd = cols_ref.shape[1], cols_ref.shape[2]
    n = blocks * sd
    lane = lax.broadcasted_iota(jnp.int32, (sd, 128), 1)
    for b in range(blocks):
        h = cols_ref[0, b]
        l = cols_ref[1, b]
        ht = h[:, 768:].astype(jnp.float32)
        lt = l[:, 768:].astype(jnp.float32)
        for f in range(3):
            hr, hi = h[:, 256 * f:256 * f + 128], h[:, 256 * f + 128:256 * f + 256]
            lr, li = l[:, 256 * f:256 * f + 128], l[:, 256 * f + 128:256 * f + 256]
            t = spread_tail(ht, lt, ht, 32 * f)
            u = jnp.where((lane & 16) == 0, -pltpu.roll(t, 112, 1), pltpu.roll(t, 16, 1))
            rhs_ref[f, b * sd:(b + 1) * sd] = jnp.concatenate([hr, hi, lr, li, hr, hi, t.astype(jnp.bfloat16)], axis=1)
            rhs_ref[f, n + b * sd:n + (b + 1) * sd] = jnp.concatenate([-hi, hr, -li, lr, -hi, hr, u.astype(jnp.bfloat16)], axis=1)

def pair_kernel(norm, cols_ref, rows_ref, out_ref, rhs_ref):
    @pl.when((pl.program_id(0) == 0))
    def _():
        prepare(cols_ref, rhs_ref)
    gb, sd = rows_ref.shape[1], rows_ref.shape[2]
    n = rhs_ref.shape[1] // 2
    h = rows_ref[0].reshape(gb * sd, -1)
    l = rows_ref[1].reshape(gb * sd, -1)
    ht = h[:, 768:].astype(jnp.float32)
    lt = l[:, 768:].astype(jnp.float32)
    for f in range(3):
        t = spread_tail(ht, ht, lt, 32 * f).astype(jnp.bfloat16)
        hm = h[:, 256 * f:256 * f + 256]
        lhs = jnp.concatenate([hm, hm, l[:, 256 * f:256 * f + 256], t], axis=1)
        p = lax.dot_general(lhs, rhs_ref[f], (((1,), (1,)), ((), ())), preferred_element_type=jnp.float32)
        p = (p * norm).astype(jnp.bfloat16)
        out_ref[f, 0] = p[:, :n]
        out_ref[f, 1] = p[:, n:]

def pair_products(rows, cols, norm, gb):
    _, nb, sd, width = rows.shape
    cb = cols.shape[1]
    n = cb * sd
    return pl.pallas_call(
        functools.partial(pair_kernel, norm),
        out_shape=jax.ShapeDtypeStruct((3, 2, nb * sd, n), jnp.bfloat16),
        grid=(nb // gb,),
        in_specs=[pl.BlockSpec((2, cb, sd, width), lambda i: (0, 0, 0, 0), pipeline_mode=pl.Buffered(1)),
                  pl.BlockSpec((2, gb, sd, width), lambda i: (0, i, 0, 0))],
        out_specs=pl.BlockSpec((3, 2, gb * sd, n), lambda i: (0, 0, i, 0)),
        scratch_shapes=[pltpu.VMEM((3, 2 * n, width), jnp.bfloat16)],
        compiler_params=pltpu.CompilerParams(vmem_limit_bytes=40 * 2**20),
        name="pair_products",
    )(cols, rows)


def shards(spectra, station_ids, counts):
    row_count = lax.axis_size("row")
    column_count = lax.axis_size("col")
    readers = row_count * column_count
    slots, segments, _ = spectra.shape
    home_rows = slots // 2
    packed = whiten_pack(spectra, station_ids, counts, readers, group=48)
    packed = packed.reshape(2, row_count, column_count, 8, 128)
    rows, cols = exchange(packed, row_count, column_count, home_rows)
    return pair_products(rows, cols, 1.0 / math.sqrt(segments), 4)


def solution(mesh):
    in_specs = (P(("row", "col"), None, None), P(("row", "col")), P(("row", "col")))
    out_specs = P(None, None, "row", "col")
    return jax.shard_map(shards, mesh=mesh, in_specs=in_specs, out_specs=out_specs, check_vma=False)
```

```python
import functools
import math

import jax
import jax.numpy as jnp
from jax import lax
from jax.experimental import pallas as pl
from jax.experimental.pallas import tpu as pltpu
from jax.sharding import PartitionSpec as P

def whiten_kernel(ids_ref, counts_ref, x_ref, out_ref, used_ref):
    first = pl.program_id(0) == 0
    step = pl.num_programs(0) - 1 - pl.program_id(0)
    group = x_ref.shape[0]
    homes = used_ref.shape[0]

    @pl.when(first)
    def _():
        out_ref[...] = jnp.zeros_like(out_ref)
        def clear(i, c):
            used_ref[i] = 0
            return c
        lax.fori_loop(0, homes, clear, 0)

    x = x_ref[...]
    x = jnp.concatenate([x[:, :128].reshape(group * 128, 128), x[:, 128:].reshape(group * 16, 128)], axis=0)
    xf = x.astype(jnp.float32)
    energy = xf * xf
    high = energy.astype(jnp.bfloat16)
    low = (energy - high.astype(jnp.float32)).astype(jnp.bfloat16)
    q = lax.broadcasted_iota(jnp.int32, (8, 128), 0)
    lane = lax.broadcasted_iota(jnp.int32, (8, 128), 1)
    start = (q // 2) * 16
    inside = (q < 6) & ((lane & 63) >= start) & ((lane & 63) < start + 32)
    window = jnp.where(inside, 1.0, 0.0).astype(jnp.bfloat16)
    center = jnp.where((q < 6) & (lane == start + 16 + (q & 1) * 64), 1.0, 0.0).astype(jnp.bfloat16)
    contract = (((1,), (1,)), ((), ()))
    total = lax.dot_general(jnp.concatenate([window, window], axis=1), jnp.concatenate([high, low], axis=1),
                            contract, preferred_element_type=jnp.float32)
    values = lax.dot_general(center, x, contract, preferred_element_type=jnp.float32)
    white = values * lax.rsqrt(jnp.maximum(total * (1.0 / 32), 0.25))

    sub = lax.broadcasted_iota(jnp.int32, (8, 128), 0)
    chunk = lax.broadcasted_iota(jnp.int32, (8, 128), 1) // 16
    for part in reversed(range(group // 8)):
        base = group * 128 + part * 128
        tail = white[:, base:base + 128]
        turned = jnp.zeros_like(tail)
        for d in range(8):
            piece = jnp.where(((chunk - sub) & 7) == d, tail, 0.0)
            if d:
                piece = pltpu.roll(pltpu.roll(piece, 128 - 16 * d, 1), d, 0)
            turned = turned + piece
        for k in reversed(range(8)):
            j = part * 8 + k
            slot = step * group + j
            station = ids_ref[slot]
            home = (station * 43691) >> 22
            live = slot < counts_ref[0]
            seen = used_ref[home]
            used_ref[home] = jnp.where(live, seen + 1, seen)
            place = jnp.where(live, seen * homes + home, 0)
            mark = (station - home * 96 + 1).astype(jnp.float32)
            tile = jnp.where(sub < 6, white[:, j * 128:(j + 1) * 128],
                             jnp.where(sub == 6, jnp.broadcast_to(turned[k:k + 1], (8, 128)), mark))
            out_ref[place] = jnp.where(live, tile, 0.0)

def whiten_pack(spectra, ids, counts, homes, group=8):
    slots, segs, width = spectra.shape
    return pl.pallas_call(
        whiten_kernel,
        out_shape=jax.ShapeDtypeStruct((2 * homes, 8, 128), jnp.float32),
        grid=(slots // group,),
        in_specs=[pl.BlockSpec(memory_space=pltpu.SMEM), pl.BlockSpec(memory_space=pltpu.SMEM),
                  pl.BlockSpec((group, segs, width), lambda i: (slots // group - 1 - i, 0, 0))],
        out_specs=pl.BlockSpec((2 * homes, 8, 128), lambda i: (0, 0, 0)),
        scratch_shapes=[pltpu.SMEM((homes,), jnp.int32)],
        compiler_params=pltpu.CompilerParams(vmem_limit_bytes=60 * 2**20),
        name="whiten_pack",
    )(ids, counts, spectra)


MESH = pl.DeviceIdType.MESH
RING = 4
X, Y = 0, 1


def arrival(half, ox, oy, q):
    axes = (X, Y) if half == 0 else (Y, X)
    off = {X: ox, Y: oy}
    for axis in (axes[1], axes[0]):
        o = off[axis]
        if o:
            return (axis, 1) if o == 3 or (o == 2 and q == 0) else (axis, -1)
    return None


def row_plan():
    left = []
    for half in (0, 1):
        axes = (X, Y) if half == 0 else (Y, X)
        for ox in range(RING):
            for oy in range(RING):
                off = {X: ox, Y: oy}
                for q in (0, 1):
                    for level, axis in enumerate(axes):
                        if level == 0 and off[axes[1]]:
                            continue
                        o = off[axis]
                        for direction in (1, -1):
                            onward = (o == 3 and direction == 1 and q == 0) or (o == 1 and direction == -1 and q == 1)
                            if o == 0 or onward:
                                left.append((level, (half, ox, oy, q, axis, direction)))
    ready = {(half, 0, 0, q): 0 for half in (0, 1) for q in (0, 1)}
    order = []
    time = 0
    while left:
        for link in ((X, 1), (X, -1), (Y, 1), (Y, -1)):
            able = [e for e in left if e[1][4:] == link and ready.get(e[1][:4], time + 1) <= time]
            if able:
                entry = min(able, key=lambda e: (ready[e[1][:4]], e[0]))
                left.remove(entry)
                order.append((time, entry[1]))
                there = beyond(entry[1])
                assert arrival(*there) == link and there not in ready
                ready[there] = time + 2
        time += 1
    whole = {}
    for (half, ox, oy, q), when in ready.items():
        whole[(ox, oy)] = max(whole.get((ox, oy), 0), when)
    return order, sorted(whole.items(), key=lambda e: (e[1], e[0]))


def beyond(item):
    half, ox, oy, q, axis, direction = item
    return (half, (ox - direction) % RING if axis == X else ox, (oy - direction) % RING if axis == Y else oy, q)


GROUPS = (4, 4, 3)


def block_groups():
    blocks = [offset for offset, when in row_plan()[1]]
    early = []
    for size in GROUPS:
        early.append(blocks[:size])
        blocks = blocks[size:]
    return early, blocks


def exchange_kernel(norm, packed_ref, rows_ref, rhs_ref, part_ref, cols_ref, mid0_ref, mid1_ref, recv0_ref, recv1_ref, own_sem, hop_send, hop_recv,
                    row_send, row_recv, col_send, col_recv):
    r = lax.axis_index("row")
    c = lax.axis_index("col")
    nr, nc = lax.axis_size("row"), lax.axis_size("col")
    x, y = c // RING, c % RING

    barrier = pltpu.get_barrier_semaphore()
    row_peers = [(r + d) % nr for d in range(1, nr)]
    col_peers = [(c + d) % nc for d in range(1, nc)]
    for p in row_peers:
        pl.semaphore_signal(barrier, inc=1, device_id=(p, c), device_id_type=MESH)
    for p in col_peers:
        pl.semaphore_signal(barrier, inc=1, device_id=(r, p), device_id_type=MESH)
    pl.semaphore_wait(barrier, nr + nc - 2)

    def send(source, target, where, k):
        pltpu.make_async_remote_copy(source, target, hop_send.at[k], hop_recv.at[k],
                                     device_id=where, device_id_type=MESH).start()

    def keep(source, target, k):
        pltpu.make_async_copy(source, target, own_sem.at[k]).start()

    def arrive(ref, count, local, k):
        others = ref.at[pl.ds(0, count)]
        pltpu.make_async_copy(others, others, hop_recv.at[k]).wait()
        pltpu.make_async_copy(local, local, own_sem.at[k]).wait()

    for p in col_peers:
        send(packed_ref.at[1, :, p], mid1_ref.at[c], (r, p), 1)
    for p in row_peers:
        send(packed_ref.at[0, p], mid0_ref.at[r], (p, c), 0)
    keep(packed_ref.at[0, r], mid0_ref.at[r], 0)
    keep(packed_ref.at[1, :, c], mid1_ref.at[c], 1)
    arrive(mid0_ref, nr - 1, mid0_ref.at[r], 0)
    for p in col_peers:
        send(mid0_ref.at[:, p], recv0_ref.at[c], (r, p), 2)
    keep(mid0_ref.at[:, c], recv0_ref.at[c], 2)
    arrive(mid1_ref, nc - 1, mid1_ref.at[c], 1)
    for p in row_peers:
        send(mid1_ref.at[:, p], recv1_ref.at[r], (p, c), 3)
    keep(mid1_ref.at[:, r], recv1_ref.at[r], 3)
    arrive(recv0_ref, nc - 1, recv0_ref.at[c], 2)
    arrive(recv1_ref, nr - 1, recv1_ref.at[r], 3)

    half_slots = nr * nc
    sd = rows_ref.shape[2]
    flat = [ref.reshape(half_slots * 8, 128) for ref in (recv0_ref, recv1_ref)]

    def plane(k):
        return jnp.concatenate([ref[pl.ds(k, half_slots, stride=8), :] for ref in flat], axis=0)

    mark = plane(7)
    lane = lax.broadcasted_iota(jnp.int32, mark.shape, 1)
    hit = jnp.where(mark == (lane + 1).astype(jnp.float32), 1.0, 0.0)
    pick = jnp.transpose(hit)[:sd].astype(jnp.bfloat16)
    for k in range(7):
        values = plane(k)
        high = values.astype(jnp.bfloat16)
        low = (values - high.astype(jnp.float32)).astype(jnp.bfloat16)
        placed = jnp.dot(pick, jnp.concatenate([high, low], axis=1),
                         preferred_element_type=jnp.float32).astype(jnp.bfloat16)
        for half in (0, 1):
            piece = placed[:, half * 128:(half + 1) * 128]
            rows_ref[half, c, :, k * 128:(k + 1) * 128] = piece
            cols_ref[half, r, :, k * 128:(k + 1) * 128] = piece

    part = sd // 2
    row_sem = {}

    def row_copy(item):
        half, ox, oy, q, axis, direction = item
        source = (x + ox) % RING * RING + (y + oy) % RING
        ref = rows_ref.at[half, source, pl.ds(q * part, part)]
        tx, ty = (x + direction) % RING, (y + direction) % RING
        target = (tx * RING + y) if axis == X else (x * RING + ty)
        index = row_sem[beyond(item)]
        return pltpu.make_async_remote_copy(ref, ref, row_send, row_recv.at[index],
                                            device_id=(r, target), device_id_type=MESH)

    def row_wait(half, ox, oy, q):
        source = (x + ox) % RING * RING + (y + oy) % RING
        ref = rows_ref.at[half, source, pl.ds(q * part, part)]
        pltpu.make_async_copy(ref, ref, row_recv.at[row_sem[(half, ox, oy, q)]]).wait()

    z, core = r // 2, r % 2
    col_sem = {}

    def col_copy(oz, q, link):
        source = (z + oz) % RING * 2 + core
        ref = cols_ref.at[:, source, pl.ds(q * part, part)]
        if link == 0:
            target = z * 2 + (1 - core)
            there = ("core", oz, q)
        else:
            target = (z + link) % RING * 2 + core
            there = ("z", (oz - link) % RING, q)
        index = col_sem.setdefault(there, len(col_sem))
        return pltpu.make_async_remote_copy(ref, ref, col_send, col_recv.at[index],
                                            device_id=(target, c), device_id_type=MESH)

    def col_wait(kind, oz, q):
        source = (z + oz) % RING * 2 + (core if kind == "z" else 1 - core)
        ref = cols_ref.at[:, source, pl.ds(q * part, part)]
        pltpu.make_async_copy(ref, ref, col_recv.at[col_sem[(kind, oz, q)]]).wait()

    order, whole = row_plan()

    def multiply(product):
        _, group, position, f = product
        for ox, oy in group:
            for half in (0, 1):
                for q in (0, 1):
                    row_ready((half, ox, oy, q))
        blocks = [(x + ox) % RING * RING + (y + oy) % RING for ox, oy in group]
        real, imag = products_of(rows_ref, rhs_ref, blocks, f, norm)
        for i in range(len(group)):
            part_ref[position + i, f, 0] = real[i * sd:(i + 1) * sd]
            part_ref[position + i, f, 1] = imag[i * sd:(i + 1) * sd]

    for _, item in order:
        row_sem.setdefault(beyond(item), len(row_sem))
    waited = set()

    def row_ready(chunk):
        if chunk in row_sem and chunk not in waited:
            row_wait(*chunk)
            waited.add(chunk)

    for q in (0, 1):
        for link in (1, -1, 0):
            col_copy(0, q, link).start()
    col_steps = {3: [("z", 3, 0, (1, 0)), ("z", 1, 0, (0,))], 5: [("z", 1, 1, (-1, 0)), ("z", 3, 1, (0,))],
                 7: [("z", 2, 0, (0,)), ("z", 2, 1, (0,))]}
    col_jobs = {0: [("z", 0)], 1: [("core", 0)], 5: [("z", 3), ("z", 1)], 6: [("core", 3), ("core", 1)],
                7: [("z", 2)], 8: [("core", 2)]}
    early, _ = block_groups()
    done_at = dict(whole)
    products = []
    position = 0
    for group in early:
        for f in range(3):
            products.append((max(done_at[b] for b in group), group, position, f))
        position += len(group)
    last = max(t for t, _ in order)

    for time in range(last + 1):
        for step in col_steps.get(time, []):
            kind, oz, q, links = step
            col_wait(kind, oz, q)
            for link in links:
                col_copy(oz, q, link).start()
        for when, item in order:
            if when == time:
                row_ready(item[:4])
                row_copy(item).start()
        for kind, oz in col_jobs.get(time, []):
            if kind == "core":
                col_wait(kind, oz, 0)
                col_wait(kind, oz, 1)
            source = (z + oz) % RING * 2 + (core if kind == "z" else 1 - core)
            prepare(cols_ref[0, source], cols_ref[1, source], rhs_ref, pl.multiple_of(source * sd, 32), nr * sd)
        if time >= 8 and products and products[0][0] <= time:
            multiply(products.pop(0))
    while products:
        multiply(products.pop(0))
    for chunk in row_sem:
        row_ready(chunk)
    for k, (ref, count) in enumerate([(mid0_ref, nr), (mid1_ref, nc), (recv0_ref, nc), (recv1_ref, nr)]):
        sent = ref.at[pl.ds(0, count - 1)]
        pltpu.make_async_copy(sent, sent, hop_send.at[k]).wait()
    sent = rows_ref.at[:, pl.ds(0, nc - 1)]
    pltpu.make_async_copy(sent, sent, row_send).wait()
    sent = cols_ref.at[:, pl.ds(0, nr - 1)]
    pltpu.make_async_copy(sent, sent, col_send).wait()


def exchange(packed, nr, nc, sd, norm):
    dma = pltpu.SemaphoreType.DMA
    n = nr * sd
    vmem = pl.BlockSpec(memory_space=pltpu.VMEM)
    return pl.pallas_call(
        functools.partial(exchange_kernel, norm),
        out_shape=(jax.ShapeDtypeStruct((2, nc, sd, 896), jnp.bfloat16),
                   jax.ShapeDtypeStruct((3, 2 * n, 896), jnp.bfloat16),
                   jax.ShapeDtypeStruct((sum(GROUPS), 3, 2, sd, n), jnp.bfloat16)),
        in_specs=[pl.BlockSpec(memory_space=pltpu.HBM)],
        out_specs=(vmem, vmem, vmem),
        scratch_shapes=[pltpu.VMEM((2, nr, sd, 896), jnp.bfloat16),
                        pltpu.VMEM((nr, nc, 8, 128), jnp.float32), pltpu.VMEM((nc, nr, 8, 128), jnp.float32),
                        pltpu.VMEM((nc, nr, 8, 128), jnp.float32), pltpu.VMEM((nr, nc, 8, 128), jnp.float32),
                        dma((4,)), dma((4,)), dma((4,)), dma, dma((60,)), dma, dma((14,))],
        compiler_params=pltpu.CompilerParams(collective_id=0, has_side_effects=True, vmem_limit_bytes=24 * 2**20),
        name="exchange",
    )(packed)


def spread_tail(first, second, third, shift):
    lane = lax.broadcasted_iota(jnp.int32, first.shape, 1)
    out = jnp.where(lane < 32, pltpu.roll(first, (128 - shift) % 128, 1), 0.0)
    out = jnp.where((lane >= 32) & (lane < 64), pltpu.roll(second, (160 - shift) % 128, 1), out)
    return jnp.where((lane >= 64) & (lane < 96), pltpu.roll(third, (192 - shift) % 128, 1), out)


def prepare(h, l, rhs_ref, at, n):
    sd = h.shape[0]
    lane = lax.broadcasted_iota(jnp.int32, (sd, 128), 1)
    ht = h[:, 768:].astype(jnp.float32)
    lt = l[:, 768:].astype(jnp.float32)
    for f in range(3):
        hr, hi = h[:, 256 * f:256 * f + 128], h[:, 256 * f + 128:256 * f + 256]
        lr, li = l[:, 256 * f:256 * f + 128], l[:, 256 * f + 128:256 * f + 256]
        t = spread_tail(ht, lt, ht, 32 * f)
        u = jnp.where((lane & 16) == 0, -pltpu.roll(t, 112, 1), pltpu.roll(t, 16, 1))
        rhs_ref[f, pl.ds(at, sd)] = jnp.concatenate([hr, hi, lr, li, hr, hi, t.astype(jnp.bfloat16)], axis=1)
        rhs_ref[f, pl.ds(at + n, sd)] = jnp.concatenate([-hi, hr, -li, lr, -hi, hr, u.astype(jnp.bfloat16)], axis=1)


def products_of(rows_ref, rhs_ref, blocks, f, norm):
    n = rhs_ref.shape[1] // 2

    def take(half, start, width):
        return jnp.concatenate([rows_ref[half, b, :, start:start + width] for b in blocks], axis=0)
    ht = take(0, 768, 128).astype(jnp.float32)
    lt = take(1, 768, 128).astype(jnp.float32)
    high = take(0, 256 * f, 256)
    lhs = jnp.concatenate([high, high, take(1, 256 * f, 256), spread_tail(ht, ht, lt, 32 * f).astype(jnp.bfloat16)], axis=1)
    p = lax.dot_general(lhs, rhs_ref[f], (((1,), (1,)), ((), ())), preferred_element_type=jnp.float32)
    p = (p * norm).astype(jnp.bfloat16)
    return p[:, :n], p[:, n:]


def finish_kernel(norm, rows_ref, rhs_ref, part_ref, out_ref, rest_ref, part_sem, rest_sem):
    c = lax.axis_index("col")
    x, y = c // RING, c % RING
    sd = rows_ref.shape[2]
    early, late = block_groups()

    def block(offset):
        return (x + offset[0]) % RING * RING + (y + offset[1]) % RING

    def rows_of(b):
        return pl.ds(pl.multiple_of(b * sd, 32), sd)

    place = [block(o) for group in early for o in group]
    for i, b in enumerate(place):
        pltpu.make_async_copy(part_ref.at[i], out_ref.at[:, :, rows_of(b)], part_sem.at[i]).start()
    blocks = [block(o) for o in late]
    for f in range(3):
        real, imag = products_of(rows_ref, rhs_ref, blocks, f, norm)
        rest_ref[f, 0] = real
        rest_ref[f, 1] = imag
        for i, b in enumerate(blocks):
            pltpu.make_async_copy(rest_ref.at[f, :, pl.ds(i * sd, sd)], out_ref.at[f, :, rows_of(b)],
                                  rest_sem.at[f, i]).start()
    for i, b in enumerate(place):
        pltpu.make_async_copy(part_ref.at[i], out_ref.at[:, :, rows_of(b)], part_sem.at[i]).wait()
    for f in range(3):
        for i, b in enumerate(blocks):
            pltpu.make_async_copy(rest_ref.at[f, :, pl.ds(i * sd, sd)], out_ref.at[f, :, rows_of(b)],
                                  rest_sem.at[f, i]).wait()


def finish(rows, rhs, part, norm):
    _, nc, sd, _ = rows.shape
    n = rhs.shape[1] // 2
    late = nc - part.shape[0]
    dma = pltpu.SemaphoreType.DMA
    vmem = pl.BlockSpec(memory_space=pltpu.VMEM)
    return pl.pallas_call(
        functools.partial(finish_kernel, norm),
        out_shape=jax.ShapeDtypeStruct((3, 2, nc * sd, n), jnp.bfloat16),
        in_specs=[vmem, vmem, vmem],
        out_specs=pl.BlockSpec(memory_space=pl.ANY),
        scratch_shapes=[pltpu.VMEM((3, 2, late * sd, n), jnp.bfloat16), dma((nc - late,)), dma((3, late))],
        compiler_params=pltpu.CompilerParams(vmem_limit_bytes=24 * 2**20),
        name="finish",
    )(rows, rhs, part)


def shards(spectra, station_ids, counts):
    row_count = lax.axis_size("row")
    column_count = lax.axis_size("col")
    readers = row_count * column_count
    slots, segments, _ = spectra.shape
    home_rows = slots // 2
    packed = whiten_pack(spectra, station_ids, counts, readers, group=48)
    packed = packed.reshape(2, row_count, column_count, 8, 128)
    norm = 1.0 / math.sqrt(segments)
    rows, rhs, part = exchange(packed, row_count, column_count, home_rows, norm)
    return finish(rows, rhs, part, norm)


def solution(mesh):
    in_specs = (P(("row", "col"), None, None), P(("row", "col")), P(("row", "col")))
    out_specs = P(None, None, "row", "col")
    return jax.shard_map(shards, mesh=mesh, in_specs=in_specs, out_specs=out_specs, check_vma=False)
```

```python
import functools
import math

import jax
import jax.numpy as jnp
from jax import lax
from jax.experimental import pallas as pl
from jax.experimental.pallas import tpu as pltpu
from jax.sharding import PartitionSpec as P

def whiten_kernel(ids_ref, counts_ref, x_ref, out_ref, used_ref):
    first = pl.program_id(0) == 0
    step = pl.num_programs(0) - 1 - pl.program_id(0)
    group = x_ref.shape[0]
    homes = used_ref.shape[0]

    @pl.when(first)
    def _():
        out_ref[...] = jnp.zeros_like(out_ref)
        def clear(i, c):
            used_ref[i] = 0
            return c
        lax.fori_loop(0, homes, clear, 0)

    x = x_ref[...]
    x = jnp.concatenate([x[:, :128].reshape(group * 128, 128), x[:, 128:].reshape(group * 16, 128)], axis=0)
    xf = x.astype(jnp.float32)
    energy = xf * xf
    high = energy.astype(jnp.bfloat16)
    low = (energy - high.astype(jnp.float32)).astype(jnp.bfloat16)
    q = lax.broadcasted_iota(jnp.int32, (8, 128), 0)
    lane = lax.broadcasted_iota(jnp.int32, (8, 128), 1)
    start = (q // 2) * 16
    inside = (q < 6) & ((lane & 63) >= start) & ((lane & 63) < start + 32)
    window = jnp.where(inside, 1.0, 0.0).astype(jnp.bfloat16)
    center = jnp.where((q < 6) & (lane == start + 16 + (q & 1) * 64), 1.0, 0.0).astype(jnp.bfloat16)
    contract = (((1,), (1,)), ((), ()))
    total = lax.dot_general(jnp.concatenate([window, window], axis=1), jnp.concatenate([high, low], axis=1),
                            contract, preferred_element_type=jnp.float32)
    values = lax.dot_general(center, x, contract, preferred_element_type=jnp.float32)
    white = values * lax.rsqrt(jnp.maximum(total * (1.0 / 32), 0.25))

    sub = lax.broadcasted_iota(jnp.int32, (8, 128), 0)
    chunk = lax.broadcasted_iota(jnp.int32, (8, 128), 1) // 16
    for part in reversed(range(group // 8)):
        base = group * 128 + part * 128
        tail = white[:, base:base + 128]
        turned = jnp.zeros_like(tail)
        for d in range(8):
            piece = jnp.where(((chunk - sub) & 7) == d, tail, 0.0)
            if d:
                piece = pltpu.roll(pltpu.roll(piece, 128 - 16 * d, 1), d, 0)
            turned = turned + piece
        for k in reversed(range(8)):
            j = part * 8 + k
            slot = step * group + j
            station = ids_ref[slot]
            home = (station * 43691) >> 22
            live = slot < counts_ref[0]
            seen = used_ref[home]
            used_ref[home] = jnp.where(live, seen + 1, seen)
            place = jnp.where(live, seen * homes + home, 0)
            mark = (station - home * 96 + 1).astype(jnp.float32)
            tile = jnp.where(sub < 6, white[:, j * 128:(j + 1) * 128],
                             jnp.where(sub == 6, jnp.broadcast_to(turned[k:k + 1], (8, 128)), mark))
            out_ref[place] = jnp.where(live, tile, 0.0)

def whiten_pack(spectra, ids, counts, homes, group=8):
    slots, segs, width = spectra.shape
    return pl.pallas_call(
        whiten_kernel,
        out_shape=jax.ShapeDtypeStruct((2 * homes, 8, 128), jnp.float32),
        grid=(slots // group,),
        in_specs=[pl.BlockSpec(memory_space=pltpu.SMEM), pl.BlockSpec(memory_space=pltpu.SMEM),
                  pl.BlockSpec((group, segs, width), lambda i: (slots // group - 1 - i, 0, 0))],
        out_specs=pl.BlockSpec((2 * homes, 8, 128), lambda i: (0, 0, 0)),
        scratch_shapes=[pltpu.SMEM((homes,), jnp.int32)],
        compiler_params=pltpu.CompilerParams(vmem_limit_bytes=60 * 2**20),
        name="whiten_pack",
    )(ids, counts, spectra)


MESH = pl.DeviceIdType.MESH
RING = 4
X, Y = 0, 1


def arrival(half, ox, oy, q):
    axes = (X, Y) if half == 0 else (Y, X)
    off = {X: ox, Y: oy}
    for axis in (axes[1], axes[0]):
        o = off[axis]
        if o:
            return (axis, 1) if o == 3 or (o == 2 and q == 0) else (axis, -1)
    return None


def row_plan():
    left = []
    for half in (0, 1):
        axes = (X, Y) if half == 0 else (Y, X)
        for ox in range(RING):
            for oy in range(RING):
                off = {X: ox, Y: oy}
                for q in (0, 1):
                    for level, axis in enumerate(axes):
                        if level == 0 and off[axes[1]]:
                            continue
                        o = off[axis]
                        for direction in (1, -1):
                            onward = (o == 3 and direction == 1 and q == 0) or (o == 1 and direction == -1 and q == 1)
                            if o == 0 or onward:
                                left.append((level, (half, ox, oy, q, axis, direction)))
    ready = {(half, 0, 0, q): 0 for half in (0, 1) for q in (0, 1)}
    order = []
    time = 0
    while left:
        for link in ((X, 1), (X, -1), (Y, 1), (Y, -1)):
            able = [e for e in left if e[1][4:] == link and ready.get(e[1][:4], time + 1) <= time]
            if able:
                entry = min(able, key=lambda e: (ready[e[1][:4]], e[0]))
                left.remove(entry)
                order.append((time, entry[1]))
                there = beyond(entry[1])
                assert arrival(*there) == link and there not in ready
                ready[there] = time + 2
        time += 1
    whole = {}
    for (half, ox, oy, q), when in ready.items():
        whole[(ox, oy)] = max(whole.get((ox, oy), 0), when)
    return order, sorted(whole.items(), key=lambda e: (e[1], e[0]))


def beyond(item):
    half, ox, oy, q, axis, direction = item
    return (half, (ox - direction) % RING if axis == X else ox, (oy - direction) % RING if axis == Y else oy, q)


GROUPS = (4, 4, 3, 2)


def block_groups():
    blocks = [offset for offset, when in row_plan()[1]]
    early = []
    for size in GROUPS:
        early.append(blocks[:size])
        blocks = blocks[size:]
    return early, blocks


def exchange_kernel(norm, packed_ref, rows_ref, rhs_ref, part_ref, cols_ref, mid0_ref, mid1_ref, recv0_ref, recv1_ref, own_sem, hop_send, hop_recv,
                    row_send, row_recv, col_send, col_recv):
    r = lax.axis_index("row")
    c = lax.axis_index("col")
    nr, nc = lax.axis_size("row"), lax.axis_size("col")
    x, y = c // RING, c % RING

    barrier = pltpu.get_barrier_semaphore()
    row_peers = [(r + d) % nr for d in range(1, nr)]
    col_peers = [(c + d) % nc for d in range(1, nc)]
    for p in row_peers:
        pl.semaphore_signal(barrier, inc=1, device_id=(p, c), device_id_type=MESH)
    for p in col_peers:
        pl.semaphore_signal(barrier, inc=1, device_id=(r, p), device_id_type=MESH)
    pl.semaphore_wait(barrier, nr + nc - 2)

    def send(source, target, where, k):
        pltpu.make_async_remote_copy(source, target, hop_send.at[k], hop_recv.at[k],
                                     device_id=where, device_id_type=MESH).start()

    def keep(source, target, k):
        pltpu.make_async_copy(source, target, own_sem.at[k]).start()

    z, core = r // 2, r % 2
    y_high, parity = y // 2, y % 2

    def columns(j):
        return [((x + dx) % RING, (y + dy) % RING) for dx in range(RING) for dy in range(j, RING, 2) if dx or dy]

    def rows_at(j):
        return [((z + dz) % RING, (core + j) % 2) for dz in range(RING) if dz or j]

    for j in (0, 1):
        h0, h1 = (parity + j) % 2, (core + j) % 2
        for px, py in columns(0) + columns(1):
            send(packed_ref.at[1, :, h1, px, py // 2, py % 2], mid1_ref.at[c, :, h1], (r, px * RING + py), 2 + j)
        for pz, pc in rows_at(0) + rows_at(1):
            send(packed_ref.at[0, pz, pc, :, :, h0], mid0_ref.at[r, :, :, h0], (pz * 2 + pc, c), j)
        keep(packed_ref.at[0, z, core, :, :, h0], mid0_ref.at[r, :, :, h0], j)
        keep(packed_ref.at[1, :, h1, x, y_high, parity], mid1_ref.at[c, :, h1], 2 + j)

    def arrive(others, local, k):
        pltpu.make_async_copy(others, others, hop_recv.at[k]).wait()
        pltpu.make_async_copy(local, local, own_sem.at[k]).wait()

    sent = []
    for j in (0, 1):
        h0, h1 = (parity + j) % 2, (core + j) % 2
        others = mid0_ref.at[pl.ds(0, nr - 1), :, :, h0]
        sent.append((others, j))
        arrive(others, mid0_ref.at[r, :, :, h0], j)
        for px, py in columns(j):
            send(mid0_ref.at[:, px, py // 2, h0], recv0_ref.at[c], (r, px * RING + py), 4)
        others = mid1_ref.at[pl.ds(0, nc - 1), :, h1]
        sent.append((others, 2 + j))
        arrive(others, mid1_ref.at[c, :, h1], 2 + j)
        for pz, pc in rows_at(j):
            send(mid1_ref.at[:, pz, h1], recv1_ref.at[r], (pz * 2 + pc, c), 5)
        if j == 0:
            keep(mid0_ref.at[:, x, y_high, parity], recv0_ref.at[c], 4)
            keep(mid1_ref.at[:, z, core], recv1_ref.at[r], 5)
    for ref, count, local, k in ((recv0_ref, nc, c, 4), (recv1_ref, nr, r, 5)):
        others = ref.at[pl.ds(0, count - 1)]
        sent.append((others, k))
        arrive(others, ref.at[local], k)

    half_slots = nr * nc
    sd = rows_ref.shape[2]
    flat = [ref.reshape(half_slots * 8, 128) for ref in (recv0_ref, recv1_ref)]

    def plane(k):
        return jnp.concatenate([ref[pl.ds(k, half_slots, stride=8), :] for ref in flat], axis=0)

    mark = plane(7)
    lane = lax.broadcasted_iota(jnp.int32, mark.shape, 1)
    hit = jnp.where(mark == (lane + 1).astype(jnp.float32), 1.0, 0.0)
    pick = jnp.transpose(hit)[:sd].astype(jnp.bfloat16)
    for k in range(7):
        values = plane(k)
        high = values.astype(jnp.bfloat16)
        low = (values - high.astype(jnp.float32)).astype(jnp.bfloat16)
        placed = jnp.dot(pick, jnp.concatenate([high, low], axis=1),
                         preferred_element_type=jnp.float32).astype(jnp.bfloat16)
        for half in (0, 1):
            piece = placed[:, half * 128:(half + 1) * 128]
            rows_ref[half, c, :, k * 128:(k + 1) * 128] = piece
            cols_ref[half, r, :, k * 128:(k + 1) * 128] = piece

    part = sd // 2
    row_sem = {}

    def row_copy(item):
        half, ox, oy, q, axis, direction = item
        source = (x + ox) % RING * RING + (y + oy) % RING
        ref = rows_ref.at[half, source, pl.ds(q * part, part)]
        tx, ty = (x + direction) % RING, (y + direction) % RING
        target = (tx * RING + y) if axis == X else (x * RING + ty)
        index = row_sem[beyond(item)]
        return pltpu.make_async_remote_copy(ref, ref, row_send, row_recv.at[index],
                                            device_id=(r, target), device_id_type=MESH)

    def row_wait(half, ox, oy, q):
        source = (x + ox) % RING * RING + (y + oy) % RING
        ref = rows_ref.at[half, source, pl.ds(q * part, part)]
        pltpu.make_async_copy(ref, ref, row_recv.at[row_sem[(half, ox, oy, q)]]).wait()

    col_sem = {}

    def col_copy(oz, q, link):
        source = (z + oz) % RING * 2 + core
        ref = cols_ref.at[:, source, pl.ds(q * part, part)]
        if link == 0:
            target = z * 2 + (1 - core)
            there = ("core", oz, q)
        else:
            target = (z + link) % RING * 2 + core
            there = ("z", (oz - link) % RING, q)
        index = col_sem.setdefault(there, len(col_sem))
        return pltpu.make_async_remote_copy(ref, ref, col_send, col_recv.at[index],
                                            device_id=(target, c), device_id_type=MESH)

    def col_wait(kind, oz, q):
        source = (z + oz) % RING * 2 + (core if kind == "z" else 1 - core)
        ref = cols_ref.at[:, source, pl.ds(q * part, part)]
        pltpu.make_async_copy(ref, ref, col_recv.at[col_sem[(kind, oz, q)]]).wait()

    order, whole = row_plan()

    def multiply(product):
        _, group, position, f = product
        for ox, oy in group:
            for half in (0, 1):
                for q in (0, 1):
                    row_ready((half, ox, oy, q))
        blocks = [(x + ox) % RING * RING + (y + oy) % RING for ox, oy in group]
        real, imag = products_of(rows_ref, rhs_ref, blocks, f, norm)
        for i in range(len(group)):
            part_ref[position + i, f, 0] = real[i * sd:(i + 1) * sd]
            part_ref[position + i, f, 1] = imag[i * sd:(i + 1) * sd]

    for _, item in order:
        row_sem.setdefault(beyond(item), len(row_sem))
    waited = set()

    def row_ready(chunk):
        if chunk in row_sem and chunk not in waited:
            row_wait(*chunk)
            waited.add(chunk)

    for q in (0, 1):
        for link in (1, -1, 0):
            col_copy(0, q, link).start()
    col_steps = {3: [("z", 3, 0, (1, 0)), ("z", 1, 0, (0,))], 5: [("z", 1, 1, (-1, 0)), ("z", 3, 1, (0,))],
                 7: [("z", 2, 0, (0,)), ("z", 2, 1, (0,))]}
    col_jobs = {0: [("z", 0)], 1: [("core", 0)], 5: [("z", 3), ("z", 1)], 6: [("core", 3), ("core", 1)],
                7: [("z", 2)], 8: [("core", 2)]}
    early, _ = block_groups()
    done_at = dict(whole)
    products = []
    position = 0
    for group in early:
        for f in range(3):
            products.append((max(done_at[b] for b in group), group, position, f))
        position += len(group)
    last = max(t for t, _ in order)

    for time in range(last + 1):
        for step in col_steps.get(time, []):
            kind, oz, q, links = step
            col_wait(kind, oz, q)
            for link in links:
                col_copy(oz, q, link).start()
        for when, item in order:
            if when == time:
                row_ready(item[:4])
                row_copy(item).start()
        for kind, oz in col_jobs.get(time, []):
            if kind == "core":
                col_wait(kind, oz, 0)
                col_wait(kind, oz, 1)
            source = (z + oz) % RING * 2 + (core if kind == "z" else 1 - core)
            prepare(cols_ref[0, source], cols_ref[1, source], rhs_ref, pl.multiple_of(source * sd, 32), nr * sd)
        if time >= 8 and products and products[0][0] <= time:
            multiply(products.pop(0))
    while products:
        multiply(products.pop(0))
    for chunk in row_sem:
        row_ready(chunk)
    for ref, k in sent:
        pltpu.make_async_copy(ref, ref, hop_send.at[k]).wait()
    sent = rows_ref.at[:, pl.ds(0, nc - 1)]
    pltpu.make_async_copy(sent, sent, row_send).wait()
    sent = cols_ref.at[:, pl.ds(0, nr - 1)]
    pltpu.make_async_copy(sent, sent, col_send).wait()


def exchange(packed, nr, nc, sd, norm):
    dma = pltpu.SemaphoreType.DMA
    n = nr * sd
    vmem = pl.BlockSpec(memory_space=pltpu.VMEM)
    return pl.pallas_call(
        functools.partial(exchange_kernel, norm),
        out_shape=(jax.ShapeDtypeStruct((2, nc, sd, 896), jnp.bfloat16),
                   jax.ShapeDtypeStruct((3, 2 * n, 896), jnp.bfloat16),
                   jax.ShapeDtypeStruct((sum(GROUPS), 3, 2, sd, n), jnp.bfloat16)),
        in_specs=[pl.BlockSpec(memory_space=pltpu.HBM)],
        out_specs=(vmem, vmem, vmem),
        scratch_shapes=[pltpu.VMEM((2, nr, sd, 896), jnp.bfloat16),
                        pltpu.VMEM((nr, RING, 2, 2, 8, 128), jnp.float32),
                        pltpu.VMEM((nc, RING, 2, 8, 128), jnp.float32),
                        pltpu.VMEM((nc, nr, 8, 128), jnp.float32), pltpu.VMEM((nr, nc, 8, 128), jnp.float32),
                        dma((6,)), dma((6,)), dma((6,)), dma, dma((60,)), dma, dma((14,))],
        compiler_params=pltpu.CompilerParams(collective_id=0, has_side_effects=True, vmem_limit_bytes=24 * 2**20),
        name="exchange",
    )(packed)


def spread_tail(first, second, third, shift):
    lane = lax.broadcasted_iota(jnp.int32, first.shape, 1)
    out = jnp.where(lane < 32, pltpu.roll(first, (128 - shift) % 128, 1), 0.0)
    out = jnp.where((lane >= 32) & (lane < 64), pltpu.roll(second, (160 - shift) % 128, 1), out)
    return jnp.where((lane >= 64) & (lane < 96), pltpu.roll(third, (192 - shift) % 128, 1), out)


def prepare(h, l, rhs_ref, at, n):
    sd = h.shape[0]
    lane = lax.broadcasted_iota(jnp.int32, (sd, 128), 1)
    ht = h[:, 768:].astype(jnp.float32)
    lt = l[:, 768:].astype(jnp.float32)
    for f in range(3):
        hr, hi = h[:, 256 * f:256 * f + 128], h[:, 256 * f + 128:256 * f + 256]
        lr, li = l[:, 256 * f:256 * f + 128], l[:, 256 * f + 128:256 * f + 256]
        t = spread_tail(ht, lt, ht, 32 * f)
        u = jnp.where((lane & 16) == 0, -pltpu.roll(t, 112, 1), pltpu.roll(t, 16, 1))
        rhs_ref[f, pl.ds(at, sd)] = jnp.concatenate([hr, hi, lr, li, hr, hi, t.astype(jnp.bfloat16)], axis=1)
        rhs_ref[f, pl.ds(at + n, sd)] = jnp.concatenate([-hi, hr, -li, lr, -hi, hr, u.astype(jnp.bfloat16)], axis=1)


def products_of(rows_ref, rhs_ref, blocks, f, norm):
    n = rhs_ref.shape[1] // 2

    def take(half, start, width):
        return jnp.concatenate([rows_ref[half, b, :, start:start + width] for b in blocks], axis=0)
    ht = take(0, 768, 128).astype(jnp.float32)
    lt = take(1, 768, 128).astype(jnp.float32)
    high = take(0, 256 * f, 256)
    lhs = jnp.concatenate([high, high, take(1, 256 * f, 256), spread_tail(ht, ht, lt, 32 * f).astype(jnp.bfloat16)], axis=1)
    p = lax.dot_general(lhs, rhs_ref[f], (((1,), (1,)), ((), ())), preferred_element_type=jnp.float32)
    p = (p * norm).astype(jnp.bfloat16)
    return p[:, :n], p[:, n:]


def finish_kernel(norm, rows_ref, rhs_ref, part_ref, out_ref, rest_ref, part_sem, rest_sem):
    c = lax.axis_index("col")
    x, y = c // RING, c % RING
    sd = rows_ref.shape[2]
    early, late = block_groups()

    def block(offset):
        return (x + offset[0]) % RING * RING + (y + offset[1]) % RING

    def rows_of(b):
        return pl.ds(pl.multiple_of(b * sd, 32), sd)

    place = [block(o) for group in early for o in group]
    for i, b in enumerate(place):
        pltpu.make_async_copy(part_ref.at[i], out_ref.at[:, :, rows_of(b)], part_sem.at[i]).start()
    blocks = [block(o) for o in late]
    for f in range(3):
        real, imag = products_of(rows_ref, rhs_ref, blocks, f, norm)
        rest_ref[f, 0] = real
        rest_ref[f, 1] = imag
        for i, b in enumerate(blocks):
            pltpu.make_async_copy(rest_ref.at[f, :, pl.ds(i * sd, sd)], out_ref.at[f, :, rows_of(b)],
                                  rest_sem.at[f, i]).start()
    for i, b in enumerate(place):
        pltpu.make_async_copy(part_ref.at[i], out_ref.at[:, :, rows_of(b)], part_sem.at[i]).wait()
    for f in range(3):
        for i, b in enumerate(blocks):
            pltpu.make_async_copy(rest_ref.at[f, :, pl.ds(i * sd, sd)], out_ref.at[f, :, rows_of(b)],
                                  rest_sem.at[f, i]).wait()


def finish(rows, rhs, part, norm):
    _, nc, sd, _ = rows.shape
    n = rhs.shape[1] // 2
    late = nc - part.shape[0]
    dma = pltpu.SemaphoreType.DMA
    vmem = pl.BlockSpec(memory_space=pltpu.VMEM)
    return pl.pallas_call(
        functools.partial(finish_kernel, norm),
        out_shape=jax.ShapeDtypeStruct((3, 2, nc * sd, n), jnp.bfloat16),
        in_specs=[vmem, vmem, vmem],
        out_specs=pl.BlockSpec(memory_space=pl.ANY),
        scratch_shapes=[pltpu.VMEM((3, 2, late * sd, n), jnp.bfloat16), dma((nc - late,)), dma((3, late))],
        compiler_params=pltpu.CompilerParams(vmem_limit_bytes=24 * 2**20),
        name="finish",
    )(rows, rhs, part)


def shards(spectra, station_ids, counts):
    row_count = lax.axis_size("row")
    column_count = lax.axis_size("col")
    readers = row_count * column_count
    slots, segments, _ = spectra.shape
    home_rows = slots // 2
    packed = whiten_pack(spectra, station_ids, counts, readers, group=48)
    packed = packed.reshape(2, RING, 2, RING, 2, 2, 8, 128)
    norm = 1.0 / math.sqrt(segments)
    rows, rhs, part = exchange(packed, row_count, column_count, home_rows, norm)
    return finish(rows, rhs, part, norm)


def solution(mesh):
    in_specs = (P(("row", "col"), None, None), P(("row", "col")), P(("row", "col")))
    out_specs = P(None, None, "row", "col")
    return jax.shard_map(shards, mesh=mesh, in_specs=in_specs, out_specs=out_specs, check_vma=False)
```

```python
import functools
import math

import jax
import jax.numpy as jnp
from jax import lax
from jax.experimental import pallas as pl
from jax.experimental.pallas import tpu as pltpu
from jax.sharding import PartitionSpec as P

SUB = 16


def whiten_kernel(ids_ref, counts_ref, x_ref, out_ref, used_ref):
    first = pl.program_id(0) == 0
    step = pl.num_programs(0) - 1 - pl.program_id(0)
    group = x_ref.shape[0]
    homes = used_ref.shape[0]

    @pl.when(first)
    def _():
        out_ref[...] = jnp.zeros_like(out_ref)
        def clear(i, c):
            used_ref[i] = 0
            return c
        lax.fori_loop(0, homes, clear, 0)

    q = lax.broadcasted_iota(jnp.int32, (8, 128), 0)
    lane = lax.broadcasted_iota(jnp.int32, (8, 128), 1)
    start = (q // 2) * 16
    inside = (q < 6) & ((lane & 63) >= start) & ((lane & 63) < start + 32)
    window = jnp.where(inside, 1.0, 0.0).astype(jnp.bfloat16)
    center = jnp.where((q < 6) & (lane == start + 16 + (q & 1) * 64), 1.0, 0.0).astype(jnp.bfloat16)
    none = jnp.zeros_like(window)
    select = jnp.concatenate([jnp.concatenate([window, none], axis=1), jnp.concatenate([none, center], axis=1)], axis=0)
    contract = (((1,), (1,)), ((), ()))
    sub = lax.broadcasted_iota(jnp.int32, (8, 128), 0)
    chunk = lax.broadcasted_iota(jnp.int32, (8, 128), 1) // 16
    def whitened(part):
        x = x_ref[part * SUB:(part + 1) * SUB]
        x = jnp.concatenate([x[:, :128].reshape(SUB * 128, 128), x[:, 128:].reshape(SUB * 16, 128)], axis=0)
        xf = x.astype(jnp.float32)
        energy = xf * xf
        energy = energy + pltpu.roll(energy, 64, 1)
        high = energy.astype(jnp.bfloat16).astype(jnp.float32)
        left = lax.broadcasted_iota(jnp.int32, energy.shape, 1) < 64
        mixed = jnp.where(left, high, energy - high).astype(jnp.bfloat16)
        both = lax.dot_general(select, jnp.concatenate([mixed, x], axis=1), contract,
                               preferred_element_type=jnp.float32)
        total, values = both[:8], both[8:]
        return values * lax.rsqrt(jnp.maximum(total * (1.0 / 32), 0.25))

    def pack(part, white):
        for eight in reversed(range(SUB // 8)):
            base = SUB * 128 + eight * 128
            tail = white[:, base:base + 128]
            turned = jnp.zeros_like(tail)
            for d in range(8):
                piece = jnp.where(((chunk - sub) & 7) == d, tail, 0.0)
                if d:
                    piece = pltpu.roll(pltpu.roll(piece, 128 - 16 * d, 1), d, 0)
                turned = turned + piece
            for k in reversed(range(8)):
                j = eight * 8 + k
                slot = step * group + part * SUB + j
                station = ids_ref[slot]
                home = (station * 43691) >> 22
                live = slot < counts_ref[0]
                seen = used_ref[home]
                used_ref[home] = jnp.where(live, seen + 1, seen)
                place = jnp.where(live, seen * homes + home, 0)
                mark = (station - home * 96 + 1).astype(jnp.float32)
                tile = jnp.where(sub < 6, white[:, j * 128:(j + 1) * 128],
                                 jnp.where(sub == 6, jnp.broadcast_to(turned[k:k + 1], (8, 128)), mark))
                out_ref[place] = jnp.where(live, tile, 0.0)

    parts = list(reversed(range(group // SUB)))
    waiting = whitened(parts[0])
    for part, following in zip(parts, parts[1:] + [None]):
        ready = waiting
        if following is not None:
            waiting = whitened(following)
        pack(part, ready)


def whiten_pack(spectra, ids, counts, homes, group=8):
    slots, segs, width = spectra.shape
    return pl.pallas_call(
        whiten_kernel,
        out_shape=jax.ShapeDtypeStruct((2 * homes, 8, 128), jnp.float32),
        grid=(slots // group,),
        in_specs=[pl.BlockSpec(memory_space=pltpu.SMEM), pl.BlockSpec(memory_space=pltpu.SMEM),
                  pl.BlockSpec((group, segs, width), lambda i: (slots // group - 1 - i, 0, 0))],
        out_specs=pl.BlockSpec((2 * homes, 8, 128), lambda i: (0, 0, 0)),
        scratch_shapes=[pltpu.SMEM((homes,), jnp.int32)],
        compiler_params=pltpu.CompilerParams(vmem_limit_bytes=50 * 2**20),
        name="whiten_pack",
    )(ids, counts, spectra)


MESH = pl.DeviceIdType.MESH
RING = 4
X, Y = 0, 1


def arrival(half, ox, oy, q):
    axes = (X, Y) if half == 0 else (Y, X)
    off = {X: ox, Y: oy}
    for axis in (axes[1], axes[0]):
        o = off[axis]
        if o:
            return (axis, 1) if o == 3 or (o == 2 and q == 0) else (axis, -1)
    return None


def row_plan():
    left = []
    for half in (0, 1):
        axes = (X, Y) if half == 0 else (Y, X)
        for ox in range(RING):
            for oy in range(RING):
                off = {X: ox, Y: oy}
                for q in (0, 1):
                    for level, axis in enumerate(axes):
                        if level == 0 and off[axes[1]]:
                            continue
                        o = off[axis]
                        for direction in (1, -1):
                            onward = (o == 3 and direction == 1 and q == 0) or (o == 1 and direction == -1 and q == 1)
                            if o == 0 or onward:
                                left.append((level, (half, ox, oy, q, axis, direction)))
    ready = {(half, 0, 0, q): 0 for half in (0, 1) for q in (0, 1)}
    order = []
    time = 0
    while left:
        for link in ((X, 1), (X, -1), (Y, 1), (Y, -1)):
            able = [e for e in left if e[1][4:] == link and ready.get(e[1][:4], time + 1) <= time]
            if able:
                entry = min(able, key=lambda e: (ready[e[1][:4]], e[0]))
                left.remove(entry)
                order.append((time, entry[1]))
                there = beyond(entry[1])
                assert arrival(*there) == link and there not in ready
                ready[there] = time + 2
        time += 1
    whole = {}
    for (half, ox, oy, q), when in ready.items():
        whole[(ox, oy)] = max(whole.get((ox, oy), 0), when)
    return order, sorted(whole.items(), key=lambda e: (e[1], e[0]))


def beyond(item):
    half, ox, oy, q, axis, direction = item
    return (half, (ox - direction) % RING if axis == X else ox, (oy - direction) % RING if axis == Y else oy, q)


GROUPS = (4, 4, 3, 2)


def block_groups():
    blocks = [offset for offset, when in row_plan()[1]]
    early = []
    for size in GROUPS:
        early.append(blocks[:size])
        blocks = blocks[size:]
    return early, blocks


def exchange_kernel(norm, packed_ref, rows_ref, rhs_ref, part_ref, cols_ref, mid0_ref, mid1_ref, recv0_ref, recv1_ref, own_sem, hop_send, hop_recv,
                    row_send, row_recv, col_send, col_recv):
    r = lax.axis_index("row")
    c = lax.axis_index("col")
    nr, nc = lax.axis_size("row"), lax.axis_size("col")
    x, y = c // RING, c % RING

    barrier = pltpu.get_barrier_semaphore()
    row_peers = [(r + d) % nr for d in range(1, nr)]
    col_peers = [(c + d) % nc for d in range(1, nc)]
    for p in row_peers:
        pl.semaphore_signal(barrier, inc=1, device_id=(p, c), device_id_type=MESH)
    for p in col_peers:
        pl.semaphore_signal(barrier, inc=1, device_id=(r, p), device_id_type=MESH)
    pl.semaphore_wait(barrier, nr + nc - 2)

    def send(source, target, where, k):
        pltpu.make_async_remote_copy(source, target, hop_send.at[k], hop_recv.at[k],
                                     device_id=where, device_id_type=MESH).start()

    def keep(source, target, k):
        pltpu.make_async_copy(source, target, own_sem.at[k]).start()

    z, core = r // 2, r % 2
    y_high, parity = y // 2, y % 2

    def columns(j):
        return [((x + dx) % RING, (y + dy) % RING) for dx in range(RING) for dy in range(j, RING, 2) if dx or dy]

    def rows_at(j):
        return [((z + dz) % RING, (core + j) % 2) for dz in range(RING) if dz or j]

    for j in (0, 1):
        h0, h1 = (parity + j) % 2, (core + j) % 2
        for px, py in columns(0) + columns(1):
            send(packed_ref.at[1, :, h1, px, py // 2, py % 2], mid1_ref.at[c, :, h1], (r, px * RING + py), 2 + j)
        for pz, pc in rows_at(0) + rows_at(1):
            send(packed_ref.at[0, pz, pc, :, :, h0], mid0_ref.at[r, :, :, h0], (pz * 2 + pc, c), j)
        keep(packed_ref.at[0, z, core, :, :, h0], mid0_ref.at[r, :, :, h0], j)
        keep(packed_ref.at[1, :, h1, x, y_high, parity], mid1_ref.at[c, :, h1], 2 + j)

    def arrive(others, local, k):
        pltpu.make_async_copy(others, others, hop_recv.at[k]).wait()
        pltpu.make_async_copy(local, local, own_sem.at[k]).wait()

    sent = []
    for j in (0, 1):
        h0, h1 = (parity + j) % 2, (core + j) % 2
        others = mid0_ref.at[pl.ds(0, nr - 1), :, :, h0]
        sent.append((others, j))
        arrive(others, mid0_ref.at[r, :, :, h0], j)
        for px, py in columns(j):
            send(mid0_ref.at[:, px, py // 2, h0], recv0_ref.at[c], (r, px * RING + py), 4)
        others = mid1_ref.at[pl.ds(0, nc - 1), :, h1]
        sent.append((others, 2 + j))
        arrive(others, mid1_ref.at[c, :, h1], 2 + j)
        for pz, pc in rows_at(j):
            send(mid1_ref.at[:, pz, h1], recv1_ref.at[r], (pz * 2 + pc, c), 5)
        if j == 0:
            keep(mid0_ref.at[:, x, y_high, parity], recv0_ref.at[c], 4)
            keep(mid1_ref.at[:, z, core], recv1_ref.at[r], 5)
    for ref, count, local, k in ((recv0_ref, nc, c, 4), (recv1_ref, nr, r, 5)):
        others = ref.at[pl.ds(0, count - 1)]
        sent.append((others, k))
        arrive(others, ref.at[local], k)

    half_slots = nr * nc
    sd = rows_ref.shape[2]
    flat = [ref.reshape(half_slots * 8, 128) for ref in (recv0_ref, recv1_ref)]

    def plane(k):
        return jnp.concatenate([ref[pl.ds(k, half_slots, stride=8), :] for ref in flat], axis=0)

    mark = plane(7)
    lane = lax.broadcasted_iota(jnp.int32, mark.shape, 1)
    hit = jnp.where(mark == (lane + 1).astype(jnp.float32), 1.0, 0.0)
    pick = jnp.transpose(hit)[:sd].astype(jnp.bfloat16)
    for k in range(7):
        values = plane(k)
        high = values.astype(jnp.bfloat16)
        low = (values - high.astype(jnp.float32)).astype(jnp.bfloat16)
        placed = jnp.dot(pick, jnp.concatenate([high, low], axis=1),
                         preferred_element_type=jnp.float32).astype(jnp.bfloat16)
        for half in (0, 1):
            piece = placed[:, half * 128:(half + 1) * 128]
            rows_ref[half, c, :, k * 128:(k + 1) * 128] = piece
            cols_ref[half, r, :, k * 128:(k + 1) * 128] = piece

    part = sd // 2
    row_sem = {}

    def row_copy(item):
        half, ox, oy, q, axis, direction = item
        source = (x + ox) % RING * RING + (y + oy) % RING
        ref = rows_ref.at[half, source, pl.ds(q * part, part)]
        tx, ty = (x + direction) % RING, (y + direction) % RING
        target = (tx * RING + y) if axis == X else (x * RING + ty)
        index = row_sem[beyond(item)]
        return pltpu.make_async_remote_copy(ref, ref, row_send, row_recv.at[index],
                                            device_id=(r, target), device_id_type=MESH)

    def row_wait(half, ox, oy, q):
        source = (x + ox) % RING * RING + (y + oy) % RING
        ref = rows_ref.at[half, source, pl.ds(q * part, part)]
        pltpu.make_async_copy(ref, ref, row_recv.at[row_sem[(half, ox, oy, q)]]).wait()

    col_sem = {}

    def col_copy(oz, q, link):
        source = (z + oz) % RING * 2 + core
        ref = cols_ref.at[:, source, pl.ds(q * part, part)]
        if link == 0:
            target = z * 2 + (1 - core)
            there = ("core", oz, q)
        else:
            target = (z + link) % RING * 2 + core
            there = ("z", (oz - link) % RING, q)
        index = col_sem.setdefault(there, len(col_sem))
        return pltpu.make_async_remote_copy(ref, ref, col_send, col_recv.at[index],
                                            device_id=(target, c), device_id_type=MESH)

    def col_wait(kind, oz, q):
        source = (z + oz) % RING * 2 + (core if kind == "z" else 1 - core)
        ref = cols_ref.at[:, source, pl.ds(q * part, part)]
        pltpu.make_async_copy(ref, ref, col_recv.at[col_sem[(kind, oz, q)]]).wait()

    order, whole = row_plan()

    def multiply(product):
        _, group, position, f = product
        for ox, oy in group:
            for half in (0, 1):
                for q in (0, 1):
                    row_ready((half, ox, oy, q))
        blocks = [(x + ox) % RING * RING + (y + oy) % RING for ox, oy in group]
        real, imag = products_of(rows_ref, rhs_ref, blocks, f, norm)
        for i in range(len(group)):
            part_ref[position + i, f, 0] = real[i * sd:(i + 1) * sd]
            part_ref[position + i, f, 1] = imag[i * sd:(i + 1) * sd]

    for _, item in order:
        row_sem.setdefault(beyond(item), len(row_sem))
    waited = set()

    def row_ready(chunk):
        if chunk in row_sem and chunk not in waited:
            row_wait(*chunk)
            waited.add(chunk)

    for q in (0, 1):
        for link in (1, -1, 0):
            col_copy(0, q, link).start()
    col_steps = {3: [("z", 3, 0, (1, 0)), ("z", 1, 0, (0,))], 5: [("z", 1, 1, (-1, 0)), ("z", 3, 1, (0,))],
                 7: [("z", 2, 0, (0,)), ("z", 2, 1, (0,))]}
    col_jobs = {0: [("z", 0)], 1: [("core", 0)], 5: [("z", 3), ("z", 1)], 6: [("core", 3), ("core", 1)],
                7: [("z", 2)], 8: [("core", 2)]}
    early, _ = block_groups()
    done_at = dict(whole)
    products = []
    position = 0
    for group in early:
        for f in range(3):
            products.append((max(done_at[b] for b in group), group, position, f))
        position += len(group)
    last = max(t for t, _ in order)

    for time in range(last + 1):
        for step in col_steps.get(time, []):
            kind, oz, q, links = step
            col_wait(kind, oz, q)
            for link in links:
                col_copy(oz, q, link).start()
        for when, item in order:
            if when == time:
                row_ready(item[:4])
                row_copy(item).start()
        for kind, oz in col_jobs.get(time, []):
            if kind == "core":
                col_wait(kind, oz, 0)
                col_wait(kind, oz, 1)
            source = (z + oz) % RING * 2 + (core if kind == "z" else 1 - core)
            prepare(cols_ref[0, source], cols_ref[1, source], rhs_ref, pl.multiple_of(source * sd, 32), nr * sd)
        if time >= 8 and products and products[0][0] <= time:
            multiply(products.pop(0))
    while products:
        multiply(products.pop(0))
    for chunk in row_sem:
        row_ready(chunk)
    for ref, k in sent:
        pltpu.make_async_copy(ref, ref, hop_send.at[k]).wait()
    sent = rows_ref.at[:, pl.ds(0, nc - 1)]
    pltpu.make_async_copy(sent, sent, row_send).wait()
    sent = cols_ref.at[:, pl.ds(0, nr - 1)]
    pltpu.make_async_copy(sent, sent, col_send).wait()


def exchange(packed, nr, nc, sd, norm):
    dma = pltpu.SemaphoreType.DMA
    n = nr * sd
    vmem = pl.BlockSpec(memory_space=pltpu.VMEM)
    return pl.pallas_call(
        functools.partial(exchange_kernel, norm),
        out_shape=(jax.ShapeDtypeStruct((2, nc, sd, 896), jnp.bfloat16),
                   jax.ShapeDtypeStruct((3, 2 * n, 896), jnp.bfloat16),
                   jax.ShapeDtypeStruct((sum(GROUPS), 3, 2, sd, n), jnp.bfloat16)),
        in_specs=[pl.BlockSpec(memory_space=pltpu.HBM)],
        out_specs=(vmem, vmem, vmem),
        scratch_shapes=[pltpu.VMEM((2, nr, sd, 896), jnp.bfloat16),
                        pltpu.VMEM((nr, RING, 2, 2, 8, 128), jnp.float32),
                        pltpu.VMEM((nc, RING, 2, 8, 128), jnp.float32),
                        pltpu.VMEM((nc, nr, 8, 128), jnp.float32), pltpu.VMEM((nr, nc, 8, 128), jnp.float32),
                        dma((6,)), dma((6,)), dma((6,)), dma, dma((60,)), dma, dma((14,))],
        compiler_params=pltpu.CompilerParams(collective_id=0, has_side_effects=True, vmem_limit_bytes=24 * 2**20),
        name="exchange",
    )(packed)


def spread_tail(first, second, third, shift):
    lane = lax.broadcasted_iota(jnp.int32, first.shape, 1)
    out = jnp.where(lane < 32, pltpu.roll(first, (128 - shift) % 128, 1), 0.0)
    out = jnp.where((lane >= 32) & (lane < 64), pltpu.roll(second, (160 - shift) % 128, 1), out)
    return jnp.where((lane >= 64) & (lane < 96), pltpu.roll(third, (192 - shift) % 128, 1), out)


def prepare(h, l, rhs_ref, at, n):
    sd = h.shape[0]
    lane = lax.broadcasted_iota(jnp.int32, (sd, 128), 1)
    ht = h[:, 768:].astype(jnp.float32)
    lt = l[:, 768:].astype(jnp.float32)
    for f in range(3):
        hr, hi = h[:, 256 * f:256 * f + 128], h[:, 256 * f + 128:256 * f + 256]
        lr, li = l[:, 256 * f:256 * f + 128], l[:, 256 * f + 128:256 * f + 256]
        t = spread_tail(ht, lt, ht, 32 * f)
        u = jnp.where((lane & 16) == 0, -pltpu.roll(t, 112, 1), pltpu.roll(t, 16, 1))
        rhs_ref[f, pl.ds(at, sd)] = jnp.concatenate([hr, hi, lr, li, hr, hi, t.astype(jnp.bfloat16)], axis=1)
        rhs_ref[f, pl.ds(at + n, sd)] = jnp.concatenate([-hi, hr, -li, lr, -hi, hr, u.astype(jnp.bfloat16)], axis=1)


def products_of(rows_ref, rhs_ref, blocks, f, norm):
    n = rhs_ref.shape[1] // 2

    def take(half, start, width):
        return jnp.concatenate([rows_ref[half, b, :, start:start + width] for b in blocks], axis=0)
    ht = take(0, 768, 128).astype(jnp.float32)
    lt = take(1, 768, 128).astype(jnp.float32)
    high = take(0, 256 * f, 256)
    lhs = jnp.concatenate([high, high, take(1, 256 * f, 256), spread_tail(ht, ht, lt, 32 * f).astype(jnp.bfloat16)], axis=1)
    p = lax.dot_general(lhs, rhs_ref[f], (((1,), (1,)), ((), ())), preferred_element_type=jnp.float32)
    p = (p * norm).astype(jnp.bfloat16)
    return p[:, :n], p[:, n:]


def finish_kernel(norm, rows_ref, rhs_ref, part_ref, out_ref, rest_ref, part_sem, rest_sem):
    c = lax.axis_index("col")
    x, y = c // RING, c % RING
    sd = rows_ref.shape[2]
    early, late = block_groups()

    def block(offset):
        return (x + offset[0]) % RING * RING + (y + offset[1]) % RING

    def rows_of(b):
        return pl.ds(pl.multiple_of(b * sd, 32), sd)

    place = [block(o) for group in early for o in group]
    for i, b in enumerate(place):
        pltpu.make_async_copy(part_ref.at[i], out_ref.at[:, :, rows_of(b)], part_sem.at[i]).start()
    blocks = [block(o) for o in late]
    for f in range(3):
        real, imag = products_of(rows_ref, rhs_ref, blocks, f, norm)
        rest_ref[f, 0] = real
        rest_ref[f, 1] = imag
        for i, b in enumerate(blocks):
            pltpu.make_async_copy(rest_ref.at[f, :, pl.ds(i * sd, sd)], out_ref.at[f, :, rows_of(b)],
                                  rest_sem.at[f, i]).start()
    for i, b in enumerate(place):
        pltpu.make_async_copy(part_ref.at[i], out_ref.at[:, :, rows_of(b)], part_sem.at[i]).wait()
    for f in range(3):
        for i, b in enumerate(blocks):
            pltpu.make_async_copy(rest_ref.at[f, :, pl.ds(i * sd, sd)], out_ref.at[f, :, rows_of(b)],
                                  rest_sem.at[f, i]).wait()


def finish(rows, rhs, part, norm):
    _, nc, sd, _ = rows.shape
    n = rhs.shape[1] // 2
    late = nc - part.shape[0]
    dma = pltpu.SemaphoreType.DMA
    vmem = pl.BlockSpec(memory_space=pltpu.VMEM)
    return pl.pallas_call(
        functools.partial(finish_kernel, norm),
        out_shape=jax.ShapeDtypeStruct((3, 2, nc * sd, n), jnp.bfloat16),
        in_specs=[vmem, vmem, vmem],
        out_specs=pl.BlockSpec(memory_space=pl.ANY),
        scratch_shapes=[pltpu.VMEM((3, 2, late * sd, n), jnp.bfloat16), dma((nc - late,)), dma((3, late))],
        compiler_params=pltpu.CompilerParams(vmem_limit_bytes=24 * 2**20),
        name="finish",
    )(rows, rhs, part)


def shards(spectra, station_ids, counts):
    row_count = lax.axis_size("row")
    column_count = lax.axis_size("col")
    readers = row_count * column_count
    slots, segments, _ = spectra.shape
    home_rows = slots // 2
    station_ids = pltpu.with_memory_space_constraint(station_ids, pltpu.HBM)
    packed = whiten_pack(spectra, station_ids, counts, readers, group=48)
    packed = packed.reshape(2, RING, 2, RING, 2, 2, 8, 128)
    norm = 1.0 / math.sqrt(segments)
    rows, rhs, part = exchange(packed, row_count, column_count, home_rows, norm)
    return finish(rows, rhs, part, norm)


def solution(mesh):
    in_specs = (P(("row", "col"), None, None), P(("row", "col")), P(("row", "col")))
    out_specs = P(None, None, "row", "col")
    return jax.shard_map(shards, mesh=mesh, in_specs=in_specs, out_specs=out_specs, check_vma=False)
```
